32 devices in a mesh: gx: 4 (over x, core), gy: 8 (over z, y).
Axes of the slice: x: 2, y: 2, z: 4, core: 2. Of those that a mesh axis runs over, the one named last changes fastest.
Arguments:
- state_field: float32 [128, 128, 16, 256], P('gx', 'gy'), may hold values from -80 to 80
- start_basis: float32 [256, 32], replicated, may hold values from -6 to 6
Outputs:
- core_tensor: float32 [128, 128, 512], P('gx', 'gy')
- z_factor: float32 [256, 32], replicated
- x_triangle: float32 [128, 128], replicated
The draws below stay inside these ranges and needn't reach their ends.
All inputs are finite; a program needn't handle non-finite values.
Results may differ from the reference program's by a relative error of at most 0.0003.
Values sent between devices are 32-bit elements; how exact they have to be, the bound alone decides.
No kernel may reach another device: no remote copies, remote signals or barrier semaphores. Data moves between devices by JAX's collectives and lax.ppermute only.
A program may use at most 64 MiB of HBM per device.

```python
import math
import jax
import jax.numpy as jnp
from jax import lax

NZ = 256
NS = 16
RZ = 32
ITERS = 3
NX = 128
NY = 128


def draw_state_field(key, part):
    noise_key = jax.random.fold_in(key, 11)
    zscale_key = jax.random.fold_in(key, 12)
    sscale_key = jax.random.fold_in(key, 13)
    noise = jax.random.truncated_normal(noise_key, -4.0, 4.0, (NX, NY, NS, NZ), jnp.float32)
    z_scale = jnp.exp(jax.random.uniform(zscale_key, (NZ,), jnp.float32, math.log(0.3), math.log(3.0)))
    s_scale = jnp.exp(jax.random.uniform(sscale_key, (NS,), jnp.float32, math.log(0.5), math.log(2.0)))
    x_ramp = jnp.exp(math.log(3.0) * jnp.arange(NX, dtype=jnp.float32) / NX)
    y_ramp = jnp.exp(math.log(3.0) * jnp.arange(NY, dtype=jnp.float32) / NY)
    amplitude = 0.3 * x_ramp[:, None] * y_ramp[None, :]
    field_values = noise * amplitude[:, :, None, None] * s_scale[None, None, :, None] * z_scale[None, None, None, :]
    return field_values


def scatter_about(key, extent, spread, limit, held_as=jnp.bfloat16):
    values = spread * jax.random.normal(key, extent, jnp.float32)
    return jnp.clip(values, min=-limit, max=limit).astype(held_as)


def setup_inputs(seed: int = 0) -> dict:
    keys = jax.random.split(jax.random.key(seed), 3)
    return {
        "state_field": draw_state_field(jax.random.fold_in(keys[2], 71), 0),
        "start_basis": scatter_about(keys[1], (NZ, RZ), 1.0, 6.0, jnp.float32),
    }


precise = lax.Precision.HIGHEST

def orthonormal(image):
    for repeat in range(2):
        inner_gram = jnp.dot(image.T.astype(jnp.float32), image.astype(jnp.float32), precision=precise, preferred_element_type=jnp.float32)
        lower_factor = jnp.linalg.cholesky(inner_gram)
        image = lax.linalg.triangular_solve(lower_factor, image, left_side=False, lower=True, transpose_a=True)
    return image

def reference(state_field, start_basis):
    unfolded = state_field.reshape(-1, NZ)
    gram_z = lax.dot_general(unfolded.astype(jnp.float32), unfolded.astype(jnp.float32), (((0,), (0,)), ((), ())), precision=precise, preferred_element_type=jnp.float32)
    z_basis = start_basis
    for iteration in range(ITERS):
        z_basis = orthonormal(jnp.dot(gram_z.astype(jnp.float32), z_basis.astype(jnp.float32), precision=precise, preferred_element_type=jnp.float32))
    core_rows = jnp.dot(unfolded.astype(jnp.float32), z_basis.astype(jnp.float32), precision=precise, preferred_element_type=jnp.float32)
    core_tensor = core_rows.reshape(NX, NY, NS * RZ)
    x_rows = core_tensor.reshape(NX, -1)
    gram_x = jnp.dot(x_rows.astype(jnp.float32), x_rows.T.astype(jnp.float32), precision=precise, preferred_element_type=jnp.float32)
    x_triangle = jnp.linalg.cholesky(gram_x).T / jnp.sqrt(jnp.float32(NY * NS * RZ))
    return (core_tensor, z_basis, x_triangle)
```

```python
import jax
import jax.numpy as jnp
from jax import lax
from jax.sharding import PartitionSpec as P

ITERS = 3


precise = lax.Precision.HIGHEST
triple = lax.Precision.HIGH


def bits(size):
    return [1 << b for b in range(size.bit_length() - 1)]


def partner(value, axis, bit):
    size = lax.axis_size(axis)
    return lax.ppermute(value, axis, [(i, i ^ bit) for i in range(size)])


def summed(value, skip_core=False):
    for axis in ("gx", "gy"):
        size = lax.axis_size(axis)
        if size & (size - 1):
            value = lax.psum(value, axis)
            continue
        for bit in bits(size)[1 if skip_core and axis == "gx" else 0 :]:
            value = value + partner(value, axis, bit)
    return value


def sum_gram(gram):
    half = gram.shape[0] // 2
    quarter = half // 2
    a, b, c = gram[:half, :half], gram[:half, half:], gram[half:, half:]
    first = jnp.concatenate([a, b[:quarter]])
    second = jnp.concatenate([c, b[quarter:]])
    upper = lax.axis_index("gx") % 2 == 0
    mine = jnp.where(upper, first, second)
    other = jnp.where(upper, second, first)
    mine = mine + partner(other, "gx", 1)
    mine = summed(mine, skip_core=True)
    other = partner(mine, "gx", 1)
    first = jnp.where(upper, mine, other)
    second = jnp.where(upper, other, mine)
    b = jnp.concatenate([first[half:], second[half:]])
    return jnp.block([[first[:half], b], [b.T, second[:half]]])


def orthonormal(image):
    for repeat in range(2):
        inner_gram = jnp.dot(image.T, image, precision=precise, preferred_element_type=jnp.float32)
        lower_factor = jnp.linalg.cholesky(inner_gram)
        image = lax.linalg.triangular_solve(
            lower_factor, image, left_side=False, lower=True, transpose_a=True
        )
    return image


def local(state_field, start_basis):
    x_cells, y_cells, species, z_cells = state_field.shape
    unfolded = state_field.reshape(x_cells * y_cells * species, z_cells)
    local_gram = lax.dot_general(
        unfolded,
        unfolded,
        (((0,), (0,)), ((), ())),
        precision=triple,
        preferred_element_type=jnp.float32,
    )
    z_basis = start_basis
    gram_z = sum_gram(local_gram)
    for iteration in range(ITERS):
        z_basis = orthonormal(
            jnp.dot(gram_z, z_basis, precision=precise, preferred_element_type=jnp.float32)
        )
    rank_kept = z_basis.shape[1]
    core_rows = jnp.dot(unfolded, z_basis, precision=triple, preferred_element_type=jnp.float32)
    core_tensor = core_rows.reshape(x_cells, y_cells, species * rank_kept)
    x_parts = lax.axis_size("gx")
    by_part = core_tensor.reshape(x_cells, x_parts, -1).transpose(1, 0, 2)
    all_x = lax.all_to_all(by_part, "gx", 0, 0).reshape(x_parts * x_cells, -1)
    product = jnp.dot(all_x, all_x.T, precision=triple, preferred_element_type=jnp.float32)
    gram_x = summed(product)
    column_count = y_cells * lax.axis_size("gy") * species * rank_kept
    x_triangle = jnp.linalg.cholesky(gram_x).T / jnp.sqrt(jnp.float32(column_count))
    return (core_tensor, z_basis, x_triangle)


def solution(mesh):
    return jax.shard_map(
        local,
        mesh=mesh,
        in_specs=(P("gx", "gy", None, None), P()),
        out_specs=(P("gx", "gy", None), P(), P()),
        check_vma=False,
    )
```

```python
import functools

import jax
import jax.numpy as jnp
from jax import lax
from jax.experimental import pallas as pl
from jax.experimental.pallas import tpu as pltpu
from jax.sharding import PartitionSpec as P

ITERS = 3
F32, BF16 = jnp.float32, jnp.bfloat16
LANES, SUBLANES = 128, 8

precise = lax.Precision.HIGHEST
ROWS_BY_ROWS = (((1,), (1,)), ((), ()))
COLUMNS_BY_COLUMNS = (((0,), (0,)), ((), ()))
VMEM = pl.BlockSpec(memory_space=pltpu.VMEM)


def bits(size):
    return [1 << b for b in range(size.bit_length() - 1)]


def partner(value, axis, mask):
    return lax.ppermute(value, axis, [(i, i ^ mask) for i in range(lax.axis_size(axis))])


def summed(value, skip_core=False):
    for axis in ("gx", "gy"):
        for bit in bits(lax.axis_size(axis))[1 if skip_core and axis == "gx" else 0 :]:
            value = value + partner(value, axis, bit)
    return value


def in_two(value):
    high = value.astype(BF16)
    return high, (value - high.astype(F32)).astype(BF16)


def tiles(value):
    rows, columns = value.shape
    return [
        [value[r : r + SUBLANES, c : min(c + LANES, columns)] for c in range(0, columns, LANES)]
        for r in range(0, rows, SUBLANES)
    ]


def joined(groups):
    return jnp.concatenate([jnp.concatenate(group, axis=1) for group in groups], axis=0)


def eliminated(gram, extra):
    gram = [list(group) for group in gram]
    extra = [list(group) for group in extra]
    row_id = lax.broadcasted_iota(jnp.int32, (SUBLANES, LANES), 0)

    def row(tile, r):
        return jnp.broadcast_to(tile[r : r + 1, :], tile.shape)

    def column(tile, c):
        return jnp.broadcast_to(tile[:, c : c + 1], (SUBLANES, LANES))

    def less(tile, factor, other):
        return tile - factor[:, : tile.shape[1]] * other

    for g in range(len(gram)):
        at, first = divmod(g * SUBLANES, LANES)
        both = [gram[h] + extra[h] for h in range(len(gram))]
        rows = [[row(t, q) for t in both[g]] for q in range(SUBLANES)]
        block = [
            [column(rows[a][at], first + b) if b >= a else None for b in range(SUBLANES)] for a in range(SUBLANES)
        ]
        below = range(g + 1, len(gram))
        columns = {h: [column(gram[h][at], first + q) for q in range(SUBLANES)] for h in below}
        scales, inverses = [], []
        for q in range(SUBLANES):
            scales.append(lax.rsqrt(block[q][q]))
            inverses.append(scales[q] * scales[q])
            for b in range(q + 1, SUBLANES):
                factor = block[q][b] * inverses[q]
                for c in range(b, SUBLANES):
                    block[b][c] = block[b][c] - factor * block[q][c]
                rows[b] = [less(t, factor, r) for t, r in zip(rows[b], rows[q])]
                for h in below:
                    columns[h][b] = columns[h][b] - factor * columns[h][q]
        for h in below:
            for q in range(SUBLANES):
                factor = columns[h][q] * inverses[q]
                both[h] = [less(t, factor, r) for t, r in zip(both[h], rows[q])]
        for q in range(SUBLANES):
            both[g] = [
                jnp.where((row_id == q)[:, : t.shape[1]], r * scales[q][:, : t.shape[1]], t)
                for t, r in zip(both[g], rows[q])
            ]
        for h in range(g, len(gram)):
            gram[h], extra[h] = both[h][: len(gram[h])], both[h][len(gram[h]) :]
    return gram, extra


def orthonormal(rows):
    for repeat in range(2):
        inner_gram = lax.dot_general(rows, rows, ROWS_BY_ROWS, precision=precise, preferred_element_type=F32)
        rows = joined(eliminated(tiles(inner_gram), tiles(rows))[1])
    return rows


def gram_kernel(field, out, square, cross):
    step = pl.program_id(0)
    high, low = in_two(field[...])
    new_square = lax.dot_general(high, high, COLUMNS_BY_COLUMNS, preferred_element_type=F32)
    new_cross = lax.dot_general(high, low, COLUMNS_BY_COLUMNS, preferred_element_type=F32)

    @pl.when(step == 0)
    def _():
        square[...] = new_square
        cross[...] = new_cross

    @pl.when(step > 0)
    def _():
        square[...] += new_square
        cross[...] += new_cross

    @pl.when(step == pl.num_programs(0) - 1)
    def _():
        half = square.shape[0] // 2
        quarter = half // 2
        full = square[...] + (cross[...] + cross[...].T)
        out[0, :half] = full[:half, :half]
        out[0, half:] = full[:quarter, half:]
        out[1, :half] = full[half:, half:]
        out[1, half:] = full[quarter:half, half:]


def local_gram(unfolded):
    rows, z = unfolded.shape
    block = rows // 2
    out = (2, z // 2 + z // 4, z // 2)
    return pl.pallas_call(
        gram_kernel,
        grid=(rows // block,),
        out_shape=jax.ShapeDtypeStruct(out, F32),
        in_specs=[pl.BlockSpec((block, z), lambda i: (i, 0))],
        out_specs=pl.BlockSpec(out, lambda i: (0, 0, 0)),
        scratch_shapes=[pltpu.VMEM((z, z), F32)] * 2,
        name="gram",
    )(unfolded)


def iterate_kernel(first, second, start, out, gram):
    half = gram.shape[0] // 2
    gram[:half, :half] = first[:half]
    gram[half:, half:] = second[:half]
    corner = jnp.concatenate([first[half:], second[half:]], axis=0)
    gram[:half, half:] = corner
    gram[half:, :half] = corner.T
    out[...] = start[...]

    @pl.loop(0, ITERS)
    def _(iteration):
        out[...] = orthonormal(jnp.dot(out[...], gram[...], precision=precise, preferred_element_type=F32))


def iterate(first, second, start_rows):
    z = start_rows.shape[1]
    return pl.pallas_call(
        iterate_kernel,
        out_shape=jax.ShapeDtypeStruct(start_rows.shape, F32),
        in_specs=[VMEM] * 3,
        out_specs=VMEM,
        scratch_shapes=[pltpu.VMEM((z, z), F32)],
        name="iterate",
    )(first, second, start_rows)


def core_kernel(species, y_cells, left, right, basis, core, by_y, weights, strip):
    rank, z = basis.shape
    cells = left.shape[0] // species
    pack = LANES // rank

    @pl.when(pl.program_id(0) == 0)
    def _():
        weights[...] = jnp.zeros_like(weights)
        for part, value in enumerate(in_two(basis[...])):
            for q in range(pack):
                weights[part * LANES + q * rank : part * LANES + (q + 1) * rank, q * z : (q + 1) * z] = value

    for t in range(species // pack):
        highs, lows = [], []
        for q in range(pack):
            for ref in (left, right):
                high, low = in_two(ref[pl.ds(t * pack + q, cells, stride=species), :])
                highs.append(high)
                lows.append(low)
        a = lax.dot_general(
            jnp.concatenate(highs, axis=1), weights[...], ROWS_BY_ROWS, preferred_element_type=F32
        )
        b = lax.dot_general(
            jnp.concatenate(lows, axis=1), weights[:LANES], ROWS_BY_ROWS, preferred_element_type=F32
        )
        strip[...] = (a[:, :LANES] + a[:, LANES:]) + b
        core[:, t * LANES : (t + 1) * LANES] = strip[...]
        for y in range(y_cells):
            by_y[y, :, t * LANES : (t + 1) * LANES] = strip[pl.ds(y, cells // y_cells, stride=y_cells), :]


def contract(unfolded, basis_rows, x_cells, y_cells, species):
    rows, z = unfolded.shape
    rank = basis_rows.shape[0]
    pack = LANES // rank
    steps = 2
    block, cells = rows // steps, rows // species // steps
    width = species * rank
    return pl.pallas_call(
        functools.partial(core_kernel, species, y_cells),
        grid=(steps,),
        out_shape=[
            jax.ShapeDtypeStruct((rows // species, width), F32),
            jax.ShapeDtypeStruct((y_cells, x_cells, width), F32),
        ],
        in_specs=[
            pl.BlockSpec((block, z // 2), lambda i: (i, 0)),
            pl.BlockSpec((block, z // 2), lambda i: (i, 1)),
            pl.BlockSpec((rank, z), lambda i: (0, 0)),
        ],
        out_specs=[
            pl.BlockSpec((cells, width), lambda i: (i, 0)),
            pl.BlockSpec((y_cells, x_cells // steps, width), lambda i: (0, i, 0)),
        ],
        scratch_shapes=[pltpu.VMEM((2 * LANES, pack * z), BF16), pltpu.VMEM((cells, LANES), F32)],
        name="core",
    )(unfolded, unfolded, basis_rows)


def product_kernel(place, *refs):
    pieces, out = refs[:-1], refs[-1]
    square = cross = 0.0
    for y in range(pieces[0].shape[0]):
        high, low = in_two(jnp.concatenate([piece[y] for piece in pieces], axis=0))
        square = square + lax.dot_general(high, high, ROWS_BY_ROWS, preferred_element_type=F32)
        cross = cross + lax.dot_general(high, low, ROWS_BY_ROWS, preferred_element_type=F32)
    total = square + (cross + cross.T)
    size = pieces[0].shape[1]
    for bit in bits(len(pieces)):
        step = size * bit
        swap = place[0] & bit != 0
        for axis in (0, 1):
            cuts = [lax.slice_in_dim(total, c, c + step, axis=axis) for c in range(0, total.shape[axis], step)]
            turned = jnp.concatenate([cuts[c ^ 1] for c in range(len(cuts))], axis=axis)
            total = jnp.where(swap, turned, total)
    out[...] = total


def product(place, pieces):
    n = len(pieces) * pieces[0].shape[1]
    return pl.pallas_call(
        product_kernel,
        out_shape=jax.ShapeDtypeStruct((n, n), F32),
        in_specs=[pl.BlockSpec(memory_space=pltpu.SMEM)] + [VMEM] * len(pieces),
        out_specs=VMEM,
        name="product",
    )(place, *pieces)


def triangle_kernel(scale, gram, out):
    upper = joined(eliminated(tiles(gram[...]), [[] for _ in range(0, gram.shape[0], SUBLANES)])[0])
    rows = lax.broadcasted_iota(jnp.int32, upper.shape, 0)
    columns = lax.broadcasted_iota(jnp.int32, upper.shape, 1)
    out[...] = jnp.where(columns >= rows, upper * scale, 0.0)


def triangle(gram, scale):
    return pl.pallas_call(
        functools.partial(triangle_kernel, scale),
        out_shape=jax.ShapeDtypeStruct(gram.shape, F32),
        in_specs=[VMEM],
        out_specs=VMEM,
        name="triangle",
    )(gram)


def local(state_field, start_basis):
    x_cells, y_cells, species, z_cells = state_field.shape
    rank_kept = start_basis.shape[1]
    unfolded = state_field.reshape(x_cells * y_cells * species, z_cells)
    halves = local_gram(unfolded)
    even = lax.axis_index("gx") % 2 == 0
    mine = jnp.where(even, halves[0], halves[1]) + partner(jnp.where(even, halves[1], halves[0]), "gx", 1)
    mine = summed(mine, skip_core=True)
    other = partner(mine, "gx", 1)
    basis_rows = iterate(jnp.where(even, mine, other), jnp.where(even, other, mine), start_basis.T)
    core_tensor, by_y = contract(unfolded, basis_rows, x_cells, y_cells, species)
    place, x_parts = lax.axis_index("gx"), lax.axis_size("gx")
    share = y_cells // x_parts
    pieces = []
    for d in range(x_parts):
        piece = lax.dynamic_slice_in_dim(by_y, (place ^ d) * share, share, axis=0)
        pieces.append(partner(piece, "gx", d) if d else piece)
    gram_x = summed(product(place.astype(jnp.int32).reshape(1), pieces))
    column_count = y_cells * lax.axis_size("gy") * species * rank_kept
    x_triangle = triangle(gram_x, 1.0 / column_count**0.5)
    return (core_tensor.reshape(x_cells, y_cells, species * rank_kept), basis_rows.T, x_triangle)


def solution(mesh):
    return jax.shard_map(
        local,
        mesh=mesh,
        in_specs=(P("gx", "gy", None, None), P()),
        out_specs=(P("gx", "gy", None), P(), P()),
        check_vma=False,
    )
```

```python
import functools

import jax
import jax.numpy as jnp
from jax import lax
from jax.experimental import pallas as pl
from jax.experimental.pallas import tpu as pltpu
from jax.sharding import PartitionSpec as P

ITERS = 3
F32, BF16 = jnp.float32, jnp.bfloat16
LANES, SUBLANES = 128, 8

precise = lax.Precision.HIGHEST
ROWS_BY_ROWS = (((1,), (1,)), ((), ()))
COLUMNS_BY_COLUMNS = (((0,), (0,)), ((), ()))
VMEM = pl.BlockSpec(memory_space=pltpu.VMEM)
SMEM = pl.BlockSpec(memory_space=pltpu.SMEM)
HBM = pl.BlockSpec(memory_space=pltpu.HBM)
SMALL = pltpu.CompilerParams(vmem_limit_bytes=32 << 20)


def bits(size):
    return [1 << b for b in range(size.bit_length() - 1)]


def partner(value, axis, mask):
    return lax.ppermute(value, axis, [(i, i ^ mask) for i in range(lax.axis_size(axis))])


def summed(value, skip_core=False):
    for axis in ("gx", "gy"):
        for bit in bits(lax.axis_size(axis))[1 if skip_core and axis == "gx" else 0 :]:
            value = value + partner(value, axis, bit)
    return value


def in_two(value):
    high = value.astype(BF16)
    return high, (value - high.astype(F32)).astype(BF16)


def tiles(value):
    rows, columns = value.shape
    return [
        [value[r : r + SUBLANES, c : min(c + LANES, columns)] for c in range(0, columns, LANES)]
        for r in range(0, rows, SUBLANES)
    ]


def joined(groups):
    return jnp.concatenate([jnp.concatenate(group, axis=1) for group in groups], axis=0)


def eliminated(gram, extra):
    gram = [list(group) for group in gram]
    extra = [list(group) for group in extra]
    row_id = lax.broadcasted_iota(jnp.int32, (SUBLANES, LANES), 0)

    def row(tile, r):
        return jnp.broadcast_to(tile[r : r + 1, :], tile.shape)

    def column(tile, c):
        return jnp.broadcast_to(tile[:, c : c + 1], (SUBLANES, LANES))

    def less(tile, factor, other):
        return tile - factor[:, : tile.shape[1]] * other

    for g in range(len(gram)):
        at, first = divmod(g * SUBLANES, LANES)
        both = [gram[h] + extra[h] for h in range(len(gram))]
        rows = [[row(t, q) for t in both[g]] for q in range(SUBLANES)]
        block = [
            [column(rows[a][at], first + b) if b >= a else None for b in range(SUBLANES)] for a in range(SUBLANES)
        ]
        below = range(g + 1, len(gram))
        columns = {h: [column(gram[h][at], first + q) for q in range(SUBLANES)] for h in below}
        scales, inverses = [], []
        for q in range(SUBLANES):
            scales.append(lax.rsqrt(block[q][q]))
            inverses.append(scales[q] * scales[q])
            for b in range(q + 1, SUBLANES):
                factor = block[q][b] * inverses[q]
                for c in range(b, SUBLANES):
                    block[b][c] = block[b][c] - factor * block[q][c]
                rows[b] = [less(t, factor, r) for t, r in zip(rows[b], rows[q])]
                for h in below:
                    columns[h][b] = columns[h][b] - factor * columns[h][q]
        for h in below:
            for q in range(SUBLANES):
                factor = columns[h][q] * inverses[q]
                both[h] = [less(t, factor, r) for t, r in zip(both[h], rows[q])]
        for q in range(SUBLANES):
            both[g] = [
                jnp.where((row_id == q)[:, : t.shape[1]], r * scales[q][:, : t.shape[1]], t)
                for t, r in zip(both[g], rows[q])
            ]
        for h in range(g, len(gram)):
            gram[h], extra[h] = both[h][: len(gram[h])], both[h][len(gram[h]) :]
    return gram, extra


def orth_pass(rows, *more):
    inner_gram = lax.dot_general(rows, rows, ROWS_BY_ROWS, precision=precise, preferred_element_type=F32)
    widths = [v.shape[1] for v in (rows, *more)]
    extra = [sum(parts, []) for parts in zip(*(tiles(v) for v in (rows, *more)))]
    groups = eliminated(tiles(inner_gram), extra)[1]
    out, at = [], 0
    for width in widths:
        count = -(-width // LANES)
        out.append(joined([group[at : at + count] for group in groups]))
        at += count
    return out


def triangle_ids(n):
    return lax.broadcasted_iota(jnp.int32, (n, n), 0), lax.broadcasted_iota(jnp.int32, (n, n), 1)


def folded(full):
    half = full.shape[0] // 2
    r, c = triangle_ids(half)
    corner = full[half:, half:]
    diagonal = jnp.sum(jnp.where(r == c, corner, 0.0), axis=0, keepdims=True)
    return jnp.where(r > c, corner, full[:half, :half]), full[:half, half:], diagonal


def opened(fold, upper, diagonal):
    half = fold.shape[0]
    r, c = triangle_ids(half)
    turned = fold.T
    first = jnp.where(c >= r, fold, turned)
    second = jnp.where(r > c, fold, jnp.where(r == c, jnp.broadcast_to(diagonal, fold.shape), turned))
    return jnp.concatenate(
        [jnp.concatenate([first, upper], axis=1), jnp.concatenate([upper.T, second], axis=1)], axis=0
    )


def species_weights(rows, repeat):
    high, low = in_two(jnp.concatenate([rows] * repeat, axis=0).T)
    weights = jnp.concatenate([high, low], axis=1)
    return jnp.concatenate([weights, weights], axis=0)


def times(value, weights):
    out = jnp.dot(jnp.concatenate(in_two(value), axis=1), weights, preferred_element_type=F32)
    half = out.shape[1] // 2
    return out[:, :half] + out[:, half:]


def packed(narrow, first, count, stride, rank):
    lane = lax.broadcasted_iota(jnp.int32, (count, LANES), 1)
    pack = LANES // rank
    out = narrow[pl.ds(first + pack - 1, count, stride=stride), :]
    for q in range(pack - 2, -1, -1):
        out = jnp.where(lane < (q + 1) * rank, narrow[pl.ds(first + q, count, stride=stride), :], out)
    return out


def gram_kernel(cuts, place, field, mine, other, held, arrived):
    copies = [
        pltpu.make_async_copy(field.at[a:b], held.at[a:b], arrived.at[i])
        for i, (a, b) in enumerate(zip(cuts[:-1], cuts[1:]))
    ]
    for copy in copies:
        copy.start()
    square = cross = 0.0
    for copy, a, b in zip(copies, cuts[:-1], cuts[1:]):
        copy.wait()
        high, low = in_two(held[a:b])
        square = square + lax.dot_general(high, high, COLUMNS_BY_COLUMNS, preferred_element_type=F32)
        cross = cross + lax.dot_general(high, low, COLUMNS_BY_COLUMNS, preferred_element_type=F32)
    fold, upper, diagonal = folded(square + (cross + cross.T))
    half = fold.shape[0]
    edge = SUBLANES
    even = place[0] & 1 == 0

    def put(first, second):
        first[:half] = fold
        first[half:] = upper[:edge]
        second[: half - edge] = upper[edge:]
        second[half - edge :] = jnp.broadcast_to(diagonal, (2 * edge, half))

    @pl.when(even)
    def _():
        put(mine, other)

    @pl.when(jnp.logical_not(even))
    def _():
        put(other, mine)


def local_gram(place, unfolded):
    rows, z = unfolded.shape
    cuts = [0, rows // 8, rows // 2, rows]
    out = jax.ShapeDtypeStruct((z // 2 + SUBLANES, z // 2), F32)
    return pl.pallas_call(
        functools.partial(gram_kernel, cuts),
        out_shape=[out, out, jax.ShapeDtypeStruct((rows, z), F32)],
        in_specs=[SMEM, HBM],
        out_specs=[VMEM] * 3,
        scratch_shapes=[pltpu.SemaphoreType.DMA((len(cuts) - 1,))],
        compiler_params=pltpu.CompilerParams(vmem_limit_bytes=32 << 20),
        name="gram",
    )(place, unfolded)


def begin_kernel(place, mine, other, start, basis, image, gram):
    half = mine.shape[1]
    edge = SUBLANES
    even = place[0] & 1 == 0
    first = jnp.where(even, mine[...], other[...])
    second = jnp.where(even, other[...], mine[...])
    gram[...] = opened(
        first[:half],
        jnp.concatenate([first[half:], second[: half - edge]], axis=0),
        second[half - edge : half - edge + 1],
    )
    basis[...] = start[...]

    def multiplied():
        return jnp.dot(basis[...], gram[...], precision=precise, preferred_element_type=F32)

    @pl.loop(0, ITERS - 2)
    def _(iteration):
        basis[...] = orth_pass(*orth_pass(multiplied()))[0]

    basis[...] = orth_pass(multiplied())[0]
    image[...] = multiplied()


def begin(place, mine, other, start_rows):
    z = start_rows.shape[1]
    rows = jax.ShapeDtypeStruct(start_rows.shape, F32)
    return pl.pallas_call(
        begin_kernel,
        out_shape=[rows, rows, jax.ShapeDtypeStruct((z, z), F32)],
        in_specs=[SMEM] + [VMEM] * 3,
        out_specs=[VMEM] * 3,
        compiler_params=SMALL,
        name="begin",
    )(place, mine, other, start_rows)


def finish_kernel(basis, gram, out, factor):
    rank = basis.shape[0]
    r, c = triangle_ids(rank)
    rows, turn = orth_pass(basis[...], jnp.where(r == c, 1.0, 0.0))
    rows = jnp.dot(rows, gram[...], precision=precise, preferred_element_type=F32)
    for repeat in range(2):
        rows, turn = orth_pass(rows, turn)
    out[...] = rows
    factor[...] = turn


def finish(basis, gram):
    rank, z = basis.shape
    return pl.pallas_call(
        finish_kernel,
        out_shape=[jax.ShapeDtypeStruct((rank, z), F32), jax.ShapeDtypeStruct((rank, rank), F32)],
        in_specs=[VMEM] * 2,
        out_specs=[VMEM] * 2,
        compiler_params=SMALL,
        cost_estimate=pl.CostEstimate(flops=1 << 30, bytes_accessed=1 << 24, transcendentals=0),
        name="finish",
    )(basis, gram)


def ahead_kernel(chunks, species, place, field, image, *refs):
    outs, narrow = refs[:-1], refs[-1]
    half = len(outs)
    share, x_cells, width = outs[0].shape
    rank = image.shape[0]
    across = half * share * species
    far = 1 - place[0] // half
    start = pl.multiple_of(far * across, across)
    step = x_cells // chunks
    weights = species_weights(image[...], LANES // rank)
    for i in range(chunks):
        cells = field[i * step : (i + 1) * step, pl.ds(start, across), :]
        narrow[...] = times(cells.reshape(step * across, cells.shape[2]), weights)
        for d, out in enumerate(outs):
            place_of_d = (place[0] ^ d) & (half - 1)
            for y in range(share):
                first = pl.multiple_of((place_of_d * share + y) * species, species)
                for t in range(width // LANES):
                    out[y, i * step : (i + 1) * step, t * LANES : (t + 1) * LANES] = packed(
                        narrow, first + t * (LANES // rank), step, across, rank
                    )


def contract_ahead(place, field, image, x_cells, y_cells, species, x_parts):
    z = field.shape[1]
    rank = image.shape[0]
    chunks = 2
    across = y_cells // 2 * species
    piece = jax.ShapeDtypeStruct((y_cells // x_parts, x_cells, species * rank), F32)
    return pl.pallas_call(
        functools.partial(ahead_kernel, chunks, species),
        out_shape=[piece] * (x_parts // 2),
        in_specs=[SMEM, VMEM, VMEM],
        out_specs=[VMEM] * (x_parts // 2),
        scratch_shapes=[pltpu.VMEM((x_cells // chunks * across, LANES), F32)],
        compiler_params=SMALL,
        name="ahead",
    )(place, field.reshape(x_cells, y_cells * species, z), image)


def core_kernel(species, y_cells, place, field, basis, core, *refs):
    outs, (weights, narrow, strip) = refs[:-3], refs[-3:]
    share, step, width = outs[0].shape
    rank = basis.shape[0]
    cells = core.shape[0]
    half = len(outs)
    near = place[0] // half * half

    @pl.when(pl.program_id(0) == 0)
    def _():
        weights[...] = species_weights(basis[...], LANES // rank)

    block = narrow.shape[0]
    narrow[...] = times(field[pl.ds(pl.multiple_of(pl.program_id(0) * block, block), block), :], weights[...])
    for t in range(width // LANES):
        lanes = slice(t * LANES, (t + 1) * LANES)
        strip[...] = packed(narrow, t * (LANES // rank), cells, species, rank)
        core[:, lanes] = strip[...]
        for d, out in enumerate(outs):
            part = near + ((place[0] ^ d) & (half - 1))
            for y in range(share):
                out[y, :, lanes] = strip[pl.ds(part * share + y, step, stride=y_cells), :]


def contract(place, unfolded, basis, x_cells, y_cells, species, x_parts):
    rows, z = unfolded.shape
    rank = basis.shape[0]
    steps = 4
    block, cells = rows // steps, rows // species // steps
    width = species * rank
    share = y_cells // x_parts
    pieces = x_parts // 2
    return pl.pallas_call(
        functools.partial(core_kernel, species, y_cells),
        grid=(steps,),
        out_shape=[jax.ShapeDtypeStruct((rows // species, width), F32)]
        + [jax.ShapeDtypeStruct((share, x_cells, width), F32)] * pieces,
        in_specs=[
            SMEM,
            VMEM,
            pl.BlockSpec((rank, z), lambda i: (0, 0)),
        ],
        out_specs=[pl.BlockSpec((cells, width), lambda i: (i, 0))]
        + [pl.BlockSpec((share, x_cells // steps, width), lambda i: (0, i, 0))] * pieces,
        scratch_shapes=[
            pltpu.VMEM((2 * z, 2 * LANES), BF16),
            pltpu.VMEM((block, LANES), F32),
            pltpu.VMEM((cells, LANES), F32),
        ],
        compiler_params=SMALL,
        cost_estimate=pl.CostEstimate(flops=1 << 31, bytes_accessed=1 << 24, transcendentals=0),
        name="core",
    )(place, unfolded, basis)


def product_kernel(place, factor, *refs):
    pieces, (out, turn) = refs[:-2], refs[-2:]
    share, size, width = pieces[0].shape
    rank = factor.shape[0]
    near, far = pieces[: len(pieces) // 2], pieces[len(pieces) // 2 :]
    turn[...] = jnp.zeros_like(turn)
    for part, value in enumerate(in_two(factor[...])):
        for side in range(2):
            for q in range(LANES // rank):
                turn[
                    part * LANES + q * rank : part * LANES + (q + 1) * rank,
                    side * LANES + q * rank : side * LANES + (q + 1) * rank,
                ] = value
    strips = [
        piece[y, :, t : t + LANES] for piece in far for y in range(share) for t in range(0, width, LANES)
    ]
    both = jnp.concatenate(in_two(jnp.concatenate(strips, axis=0)), axis=1)
    turned = lax.dot_general(both, turn[...], ROWS_BY_ROWS, preferred_element_type=F32)
    turned = turned[:, :LANES] + turned[:, LANES:]
    count = width // LANES
    square = cross = 0.0
    for y in range(share):
        rows = [piece[y] for piece in near]
        for d in range(len(far)):
            at = (d * share + y) * count
            rows.append(
                jnp.concatenate([turned[(at + t) * size : (at + t + 1) * size] for t in range(count)], axis=1)
            )
        high, low = in_two(jnp.concatenate(rows, axis=0))
        square = square + lax.dot_general(high, high, ROWS_BY_ROWS, preferred_element_type=F32)
        cross = cross + lax.dot_general(high, low, ROWS_BY_ROWS, preferred_element_type=F32)
    total = square + (cross + cross.T)
    for bit in bits(len(pieces)):
        step = size * bit
        swap = place[0] & bit != 0
        for axis in (0, 1):
            parts = [lax.slice_in_dim(total, c, c + step, axis=axis) for c in range(0, total.shape[axis], step)]
            swapped = jnp.concatenate([parts[c ^ 1] for c in range(len(parts))], axis=axis)
            total = jnp.where(swap, swapped, total)
    fold, upper, diagonal = folded(total)
    half = fold.shape[0]
    out[:half] = jnp.concatenate([fold, upper], axis=1)
    out[half:] = jnp.broadcast_to(jnp.concatenate([diagonal, diagonal], axis=1), (SUBLANES, 2 * half))


def product(place, factor, pieces):
    n = len(pieces) * pieces[0].shape[1]
    return pl.pallas_call(
        product_kernel,
        out_shape=jax.ShapeDtypeStruct((n // 2 + SUBLANES, n), F32),
        in_specs=[SMEM] + [VMEM] * (len(pieces) + 1),
        out_specs=VMEM,
        scratch_shapes=[pltpu.VMEM((2 * LANES, 2 * LANES), BF16)],
        compiler_params=SMALL,
        name="product",
    )(place, factor, *pieces)


def triangle_kernel(scale, gram, out):
    half = gram.shape[1] // 2
    full = opened(gram[:half, :half], gram[:half, half:], gram[half : half + 1, :half])
    upper = joined(eliminated(tiles(full), [[] for _ in range(0, 2 * half, SUBLANES)])[0])
    r, c = triangle_ids(2 * half)
    out[...] = jnp.where(c >= r, upper * scale, 0.0)


def triangle(gram, scale):
    n = gram.shape[1]
    return pl.pallas_call(
        functools.partial(triangle_kernel, scale),
        out_shape=jax.ShapeDtypeStruct((n, n), F32),
        in_specs=[VMEM],
        out_specs=VMEM,
        compiler_params=SMALL,
        name="triangle",
    )(gram)


def local(state_field, start_basis):
    x_cells, y_cells, species, z_cells = state_field.shape
    rank_kept = start_basis.shape[1]
    unfolded = state_field.reshape(x_cells * y_cells * species, z_cells)
    x_parts = lax.axis_size("gx")
    place = lax.axis_index("gx").astype(jnp.int32).reshape(1)
    mine, other, held = local_gram(place, pltpu.with_memory_space_constraint(unfolded, pltpu.HBM))
    mine = summed(mine + partner(other, "gx", 1), skip_core=True)
    other = partner(mine, "gx", 1)
    basis, image, gram = begin(place, mine, other, start_basis.T)
    ahead = contract_ahead(place, held, image, x_cells, y_cells, species, x_parts)
    far = [partner(piece, "gx", d + x_parts // 2) for d, piece in enumerate(ahead)]
    basis, ahead = lax.optimization_barrier((basis, ahead))
    basis_rows, factor = finish(basis, gram)
    core_tensor, *near = contract(place, held, basis_rows, x_cells, y_cells, species, x_parts)
    near = [partner(piece, "gx", d) if d else piece for d, piece in enumerate(near)]
    gram_x = summed(product(place, factor, near + far))
    column_count = y_cells * lax.axis_size("gy") * species * rank_kept
    x_triangle = triangle(gram_x, 1.0 / column_count**0.5)
    return (core_tensor.reshape(x_cells, y_cells, species * rank_kept), basis_rows.T, x_triangle)


def solution(mesh):
    return jax.shard_map(
        local,
        mesh=mesh,
        in_specs=(P("gx", "gy", None, None), P()),
        out_specs=(P("gx", "gy", None), P(), P()),
        check_vma=False,
    )
```

```python
import functools

import jax
import jax.numpy as jnp
from jax import lax
from jax.experimental import pallas as pl
from jax.experimental.pallas import tpu as pltpu
from jax.sharding import PartitionSpec as P


ITERS = 3
F32, BF16 = jnp.float32, jnp.bfloat16
LANES, SUBLANES = 128, 8

precise = lax.Precision.HIGHEST
ROWS_BY_ROWS = (((1,), (1,)), ((), ()))
COLUMNS_BY_COLUMNS = (((0,), (0,)), ((), ()))
VMEM = pl.BlockSpec(memory_space=pltpu.VMEM)
SMEM = pl.BlockSpec(memory_space=pltpu.SMEM)
HBM = pl.BlockSpec(memory_space=pltpu.HBM)
SMALL = pltpu.CompilerParams(vmem_limit_bytes=32 << 20)


def bits(size):
    return [1 << b for b in range(size.bit_length() - 1)]


def partner(value, x_mask, y_mask=0):
    x_size, y_size = lax.axis_size("gx"), lax.axis_size("gy")
    pairs = [
        (x * y_size + y, (x ^ x_mask) * y_size + (y ^ y_mask)) for x in range(x_size) for y in range(y_size)
    ]
    return lax.ppermute(value, ("gx", "gy"), pairs)


def summed(value):
    masks = [(bit, 0) for bit in bits(lax.axis_size("gx"))[1:]] + [(0, bit) for bit in bits(lax.axis_size("gy"))]
    while masks:
        first, masks = masks[0], masks[1:]
        near = value + partner(value, *first)
        if masks:
            second, masks = masks[0], masks[1:]
            both = (first[0] ^ second[0], first[1] ^ second[1])
            near = near + (partner(value, *second) + partner(value, *both))
        value = near
    return value


def in_two(value):
    high = value.astype(BF16)
    return high, (value - high.astype(F32)).astype(BF16)


def tiles(value):
    rows, columns = value.shape
    return [
        [value[r : r + SUBLANES, c : min(c + LANES, columns)] for c in range(0, columns, LANES)]
        for r in range(0, rows, SUBLANES)
    ]


def joined(groups):
    return jnp.concatenate([jnp.concatenate(group, axis=1) for group in groups], axis=0)


def eliminated(gram, extra):
    gram = [list(group) for group in gram]
    extra = [list(group) for group in extra]
    row_id = lax.broadcasted_iota(jnp.int32, (SUBLANES, LANES), 0)

    def row(tile, r):
        return jnp.broadcast_to(tile[r : r + 1, :], tile.shape)

    def column(tile, c):
        return jnp.broadcast_to(tile[:, c : c + 1], (SUBLANES, LANES))

    def less(tile, factor, other):
        return tile - factor[:, : tile.shape[1]] * other

    for g in range(len(gram)):
        at, first = divmod(g * SUBLANES, LANES)
        both = [gram[h] + extra[h] for h in range(len(gram))]
        rows = [[row(t, q) for t in both[g]] for q in range(SUBLANES)]
        block = [
            [column(rows[a][at], first + b) if b >= a else None for b in range(SUBLANES)] for a in range(SUBLANES)
        ]
        below = range(g + 1, len(gram))
        columns = {h: [column(gram[h][at], first + q) for q in range(SUBLANES)] for h in below}
        scales, inverses = [], []
        for q in range(SUBLANES):
            scales.append(lax.rsqrt(block[q][q]))
            inverses.append(scales[q] * scales[q])
            for b in range(q + 1, SUBLANES):
                factor = block[q][b] * inverses[q]
                for c in range(b, SUBLANES):
                    block[b][c] = block[b][c] - factor * block[q][c]
                rows[b] = [less(t, factor, r) for t, r in zip(rows[b], rows[q])]
                for h in below:
                    columns[h][b] = columns[h][b] - factor * columns[h][q]
        for h in below:
            for q in range(SUBLANES):
                factor = columns[h][q] * inverses[q]
                both[h] = [less(t, factor, r) for t, r in zip(both[h], rows[q])]
        for q in range(SUBLANES):
            both[g] = [
                jnp.where((row_id == q)[:, : t.shape[1]], r * scales[q][:, : t.shape[1]], t)
                for t, r in zip(both[g], rows[q])
            ]
        for h in range(g, len(gram)):
            gram[h], extra[h] = both[h][: len(gram[h])], both[h][len(gram[h]) :]
    return gram, extra


def orth_pass(rows, *more):
    inner_gram = lax.dot_general(rows, rows, ROWS_BY_ROWS, precision=precise, preferred_element_type=F32)
    widths = [v.shape[1] for v in (rows, *more)]
    extra = [sum(parts, []) for parts in zip(*(tiles(v) for v in (rows, *more)))]
    groups = eliminated(tiles(inner_gram), extra)[1]
    out, at = [], 0
    for width in widths:
        count = -(-width // LANES)
        out.append(joined([group[at : at + count] for group in groups]))
        at += count
    return out


def triangle_ids(n):
    return lax.broadcasted_iota(jnp.int32, (n, n), 0), lax.broadcasted_iota(jnp.int32, (n, n), 1)


def folded(full):
    half = full.shape[0] // 2
    r, c = triangle_ids(half)
    corner = full[half:, half:]
    diagonal = jnp.sum(jnp.where(r == c, corner, 0.0), axis=0, keepdims=True)
    return jnp.where(r > c, corner, full[:half, :half]), full[:half, half:], diagonal


def opened(fold, upper, diagonal):
    half = fold.shape[0]
    r, c = triangle_ids(half)
    turned = fold.T
    first = jnp.where(c >= r, fold, turned)
    second = jnp.where(r > c, fold, jnp.where(r == c, jnp.broadcast_to(diagonal, fold.shape), turned))
    return jnp.concatenate(
        [jnp.concatenate([first, upper], axis=1), jnp.concatenate([upper.T, second], axis=1)], axis=0
    )


def species_weights(rows, repeat):
    high, low = in_two(jnp.concatenate([rows] * repeat, axis=0).T)
    weights = jnp.concatenate([high, low], axis=1)
    return jnp.concatenate([weights, weights], axis=0)


def times(value, weights):
    out = jnp.dot(jnp.concatenate(in_two(value), axis=1), weights, preferred_element_type=F32)
    half = out.shape[1] // 2
    return out[:, :half] + out[:, half:]


def packed(narrow, first, count, stride, rank):
    lane = lax.broadcasted_iota(jnp.int32, (count, LANES), 1)
    pack = LANES // rank
    out = narrow[pl.ds(first + pack - 1, count, stride=stride), :]
    for q in range(pack - 2, -1, -1):
        out = jnp.where(lane < (q + 1) * rank, narrow[pl.ds(first + q, count, stride=stride), :], out)
    return out


def gram_kernel(cuts, place, field, mine, other, held, arrived):
    copies = [
        pltpu.make_async_copy(field.at[a:b], held.at[a:b], arrived.at[i])
        for i, (a, b) in enumerate(zip(cuts[:-1], cuts[1:]))
    ]
    for copy in copies:
        copy.start()
    square = cross = 0.0
    for copy, a, b in zip(copies, cuts[:-1], cuts[1:]):
        copy.wait()
        high, low = in_two(held[a:b])
        square = square + lax.dot_general(high, high, COLUMNS_BY_COLUMNS, preferred_element_type=F32)
        cross = cross + lax.dot_general(high, low, COLUMNS_BY_COLUMNS, preferred_element_type=F32)
    fold, upper, diagonal = folded(square + (cross + cross.T))
    half = fold.shape[0]
    edge = SUBLANES
    even = place[0] & 1 == 0

    def put(first, second):
        first[:half] = fold
        first[half:] = upper[:edge]
        second[: half - edge] = upper[edge:]
        second[half - edge :] = jnp.broadcast_to(diagonal, (2 * edge, half))

    @pl.when(even)
    def _():
        put(mine, other)

    @pl.when(jnp.logical_not(even))
    def _():
        put(other, mine)


def local_gram(place, unfolded):
    rows, z = unfolded.shape
    cuts = [0, rows // 8, rows // 2, rows]
    out = jax.ShapeDtypeStruct((z // 2 + SUBLANES, z // 2), F32)
    return pl.pallas_call(
        functools.partial(gram_kernel, cuts),
        out_shape=[out, out, jax.ShapeDtypeStruct((rows, z), F32)],
        in_specs=[SMEM, HBM],
        out_specs=[VMEM] * 3,
        scratch_shapes=[pltpu.SemaphoreType.DMA((len(cuts) - 1,))],
        compiler_params=pltpu.CompilerParams(vmem_limit_bytes=32 << 20),
        name="gram",
    )(place, unfolded)


def begin_kernel(place, mine, other, start, basis, image, gram):
    half = mine.shape[1]
    edge = SUBLANES
    even = place[0] & 1 == 0
    first = jnp.where(even, mine[...], other[...])
    second = jnp.where(even, other[...], mine[...])
    gram[...] = opened(
        first[:half],
        jnp.concatenate([first[half:], second[: half - edge]], axis=0),
        second[half - edge : half - edge + 1],
    )
    basis[...] = start[...]

    def multiplied():
        return jnp.dot(basis[...], gram[...], precision=precise, preferred_element_type=F32)

    @pl.loop(0, ITERS - 2)
    def _(iteration):
        basis[...] = orth_pass(*orth_pass(multiplied()))[0]

    basis[...] = orth_pass(multiplied())[0]
    image[...] = multiplied()


def begin(place, mine, other, start_rows):
    z = start_rows.shape[1]
    rows = jax.ShapeDtypeStruct(start_rows.shape, F32)
    return pl.pallas_call(
        begin_kernel,
        out_shape=[rows, rows, jax.ShapeDtypeStruct((z, z), F32)],
        in_specs=[SMEM] + [VMEM] * 3,
        out_specs=[VMEM] * 3,
        compiler_params=SMALL,
        name="begin",
    )(place, mine, other, start_rows)


def finish_kernel(basis, gram, out, factor):
    rank = basis.shape[0]
    r, c = triangle_ids(rank)
    rows, turn = orth_pass(basis[...], jnp.where(r == c, 1.0, 0.0))
    rows = jnp.dot(rows, gram[...], precision=precise, preferred_element_type=F32)
    for _ in range(2):
        rows, turn = orth_pass(rows, turn)
    out[...] = rows
    factor[...] = turn


def finish(basis, gram):
    rank, z = basis.shape
    return pl.pallas_call(
        finish_kernel,
        out_shape=[jax.ShapeDtypeStruct((rank, z), F32), jax.ShapeDtypeStruct((rank, rank), F32)],
        in_specs=[VMEM] * 2,
        out_specs=[VMEM] * 2,
        compiler_params=SMALL,
        cost_estimate=pl.CostEstimate(flops=1 << 30, bytes_accessed=1 << 24, transcendentals=0),
        name="finish",
    )(basis, gram)


def ahead_kernel(chunks, species, place, field, image, *refs):
    outs, narrow = refs[:-1], refs[-1]
    half = len(outs)
    share, x_cells, width = outs[0].shape
    rank = image.shape[0]
    across = half * share * species
    far = 1 - place[0] // half
    start = pl.multiple_of(far * across, across)
    step = x_cells // chunks
    weights = species_weights(image[...], LANES // rank)
    for i in range(chunks):
        cells = field[i * step : (i + 1) * step, pl.ds(start, across), :]
        narrow[...] = times(cells.reshape(step * across, cells.shape[2]), weights)
        for d, out in enumerate(outs):
            place_of_d = (place[0] ^ d) & (half - 1)
            for y in range(share):
                first = pl.multiple_of((place_of_d * share + y) * species, species)
                for t in range(width // LANES):
                    out[y, i * step : (i + 1) * step, t * LANES : (t + 1) * LANES] = packed(
                        narrow, first + t * (LANES // rank), step, across, rank
                    )


def contract_ahead(place, field, image, x_cells, y_cells, species, x_parts):
    z = field.shape[1]
    rank = image.shape[0]
    chunks = 2
    across = y_cells // 2 * species
    piece = jax.ShapeDtypeStruct((y_cells // x_parts, x_cells, species * rank), F32)
    return pl.pallas_call(
        functools.partial(ahead_kernel, chunks, species),
        out_shape=[piece] * (x_parts // 2),
        in_specs=[SMEM, VMEM, VMEM],
        out_specs=[VMEM] * (x_parts // 2),
        scratch_shapes=[pltpu.VMEM((x_cells // chunks * across, LANES), F32)],
        compiler_params=SMALL,
        name="ahead",
    )(place, field.reshape(x_cells, y_cells * species, z), image)


def core_kernel(species, y_cells, place, field, basis, core, *refs):
    outs, (weights, narrow, strip) = refs[:-3], refs[-3:]
    share, step, width = outs[0].shape
    rank = basis.shape[0]
    cells = core.shape[0]
    half = len(outs)
    near = place[0] // half * half

    @pl.when(pl.program_id(0) == 0)
    def _():
        weights[...] = species_weights(basis[...], LANES // rank)

    block = narrow.shape[0]
    narrow[...] = times(field[pl.ds(pl.multiple_of(pl.program_id(0) * block, block), block), :], weights[...])
    for t in range(width // LANES):
        lanes = slice(t * LANES, (t + 1) * LANES)
        strip[...] = packed(narrow, t * (LANES // rank), cells, species, rank)
        core[:, lanes] = strip[...]
        for d, out in enumerate(outs):
            part = near + ((place[0] ^ d) & (half - 1))
            for y in range(share):
                out[y, :, lanes] = strip[pl.ds(part * share + y, step, stride=y_cells), :]


def contract(place, unfolded, basis, x_cells, y_cells, species, x_parts):
    rows, z = unfolded.shape
    rank = basis.shape[0]
    steps = 4
    block, cells = rows // steps, rows // species // steps
    width = species * rank
    share = y_cells // x_parts
    pieces = x_parts // 2
    return pl.pallas_call(
        functools.partial(core_kernel, species, y_cells),
        grid=(steps,),
        out_shape=[jax.ShapeDtypeStruct((rows // species, width), F32)]
        + [jax.ShapeDtypeStruct((share, x_cells, width), F32)] * pieces,
        in_specs=[
            SMEM,
            VMEM,
            pl.BlockSpec((rank, z), lambda i: (0, 0)),
        ],
        out_specs=[pl.BlockSpec((cells, width), lambda i: (i, 0))]
        + [pl.BlockSpec((share, x_cells // steps, width), lambda i: (0, i, 0))] * pieces,
        scratch_shapes=[
            pltpu.VMEM((2 * z, 2 * LANES), BF16),
            pltpu.VMEM((block, LANES), F32),
            pltpu.VMEM((cells, LANES), F32),
        ],
        compiler_params=SMALL,
        cost_estimate=pl.CostEstimate(flops=1 << 31, bytes_accessed=1 << 24, transcendentals=0),
        name="core",
    )(place, unfolded, basis)


def product_kernel(place, factor, *refs):
    pieces, (out, turn) = refs[:-2], refs[-2:]
    share, size, width = pieces[0].shape
    rank = factor.shape[0]
    near, far = pieces[: len(pieces) // 2], pieces[len(pieces) // 2 :]
    turn[...] = jnp.zeros_like(turn)
    for part, value in enumerate(in_two(factor[...])):
        for side in range(2):
            for q in range(LANES // rank):
                turn[
                    part * LANES + q * rank : part * LANES + (q + 1) * rank,
                    side * LANES + q * rank : side * LANES + (q + 1) * rank,
                ] = value
    strips = [
        piece[y, :, t : t + LANES] for piece in far for y in range(share) for t in range(0, width, LANES)
    ]
    both = jnp.concatenate(in_two(jnp.concatenate(strips, axis=0)), axis=1)
    turned = lax.dot_general(both, turn[...], ROWS_BY_ROWS, preferred_element_type=F32)
    turned = turned[:, :LANES] + turned[:, LANES:]
    count = width // LANES
    square = cross = 0.0
    for y in range(share):
        rows = [piece[y] for piece in near]
        for d in range(len(far)):
            at = (d * share + y) * count
            rows.append(
                jnp.concatenate([turned[(at + t) * size : (at + t + 1) * size] for t in range(count)], axis=1)
            )
        high, low = in_two(jnp.concatenate(rows, axis=0))
        square = square + lax.dot_general(high, high, ROWS_BY_ROWS, preferred_element_type=F32)
        cross = cross + lax.dot_general(high, low, ROWS_BY_ROWS, preferred_element_type=F32)
    total = square + (cross + cross.T)
    for bit in bits(len(pieces)):
        step = size * bit
        swap = place[0] & bit != 0
        for axis in (0, 1):
            parts = [lax.slice_in_dim(total, c, c + step, axis=axis) for c in range(0, total.shape[axis], step)]
            swapped = jnp.concatenate([parts[c ^ 1] for c in range(len(parts))], axis=axis)
            total = jnp.where(swap, swapped, total)
    fold, upper, diagonal = folded(total)
    half = fold.shape[0]
    out[:half] = jnp.concatenate([fold, upper], axis=1)
    out[half:] = jnp.broadcast_to(jnp.concatenate([diagonal, diagonal], axis=1), (SUBLANES, 2 * half))


def product(place, factor, pieces):
    n = len(pieces) * pieces[0].shape[1]
    return pl.pallas_call(
        product_kernel,
        out_shape=jax.ShapeDtypeStruct((n // 2 + SUBLANES, n), F32),
        in_specs=[SMEM] + [VMEM] * (len(pieces) + 1),
        out_specs=VMEM,
        scratch_shapes=[pltpu.VMEM((2 * LANES, 2 * LANES), BF16)],
        compiler_params=SMALL,
        name="product",
    )(place, factor, *pieces)


def triangle_kernel(scale, gram, out):
    half = gram.shape[1] // 2
    full = opened(gram[:half, :half], gram[:half, half:], gram[half : half + 1, :half])
    upper = joined(eliminated(tiles(full), [[] for _ in range(0, 2 * half, SUBLANES)])[0])
    r, c = triangle_ids(2 * half)
    out[...] = jnp.where(c >= r, upper * scale, 0.0)


def triangle(gram, scale):
    n = gram.shape[1]
    return pl.pallas_call(
        functools.partial(triangle_kernel, scale),
        out_shape=jax.ShapeDtypeStruct((n, n), F32),
        in_specs=[VMEM],
        out_specs=VMEM,
        compiler_params=SMALL,
        name="triangle",
    )(gram)


def local(state_field, start_basis):
    x_cells, y_cells, species, z_cells = state_field.shape
    rank_kept = start_basis.shape[1]
    unfolded = state_field.reshape(x_cells * y_cells * species, z_cells)
    x_parts = lax.axis_size("gx")
    place = lax.axis_index("gx").astype(jnp.int32).reshape(1)
    mine, other, held = local_gram(place, pltpu.with_memory_space_constraint(unfolded, pltpu.HBM))
    mine = summed(mine + partner(other, 1))
    other = partner(mine, 1)
    basis, image, gram = begin(place, mine, other, start_basis.T)
    ahead = contract_ahead(place, held, image, x_cells, y_cells, species, x_parts)
    far = [partner(piece, d + x_parts // 2) for d, piece in enumerate(ahead)]
    basis_rows, factor = finish(basis, gram)
    core_tensor, *near = contract(place, held, basis_rows, x_cells, y_cells, species, x_parts)
    near = [partner(piece, d) if d else piece for d, piece in enumerate(near)]
    gram_x = product(place, factor, near + far)
    gram_x = summed(gram_x + partner(gram_x, 1))
    column_count = y_cells * lax.axis_size("gy") * species * rank_kept
    x_triangle = triangle(gram_x, 1.0 / column_count**0.5)
    return (core_tensor.reshape(x_cells, y_cells, species * rank_kept), basis_rows.T, x_triangle)


def solution(mesh):
    return jax.shard_map(
        local,
        mesh=mesh,
        in_specs=(P("gx", "gy", None, None), P()),
        out_specs=(P("gx", "gy", None), P(), P()),
        check_vma=False,
    )
```

```python
import functools

import jax
import jax.numpy as jnp
from jax import lax
from jax.experimental import pallas as pl
from jax.experimental.pallas import tpu as pltpu
from jax.sharding import PartitionSpec as P


ITERS = 3
F32, BF16 = jnp.float32, jnp.bfloat16
LANES, SUBLANES = 128, 8

precise = lax.Precision.HIGHEST
ROWS_BY_ROWS = (((1,), (1,)), ((), ()))
COLUMNS_BY_COLUMNS = (((0,), (0,)), ((), ()))
VMEM = pl.BlockSpec(memory_space=pltpu.VMEM)
SMEM = pl.BlockSpec(memory_space=pltpu.SMEM)
HBM = pl.BlockSpec(memory_space=pltpu.HBM)
SMALL = pltpu.CompilerParams(vmem_limit_bytes=32 << 20)


def bits(size):
    return [1 << b for b in range(size.bit_length() - 1)]


def partner(value, x_mask, y_mask=0):
    x_size, y_size = lax.axis_size("gx"), lax.axis_size("gy")
    pairs = [
        (x * y_size + y, (x ^ x_mask) * y_size + (y ^ y_mask)) for x in range(x_size) for y in range(y_size)
    ]
    return lax.ppermute(value, ("gx", "gy"), pairs)


def summed(value):
    masks = [(bit, 0) for bit in bits(lax.axis_size("gx"))[1:]] + [(0, bit) for bit in bits(lax.axis_size("gy"))]
    while masks:
        first, masks = masks[0], masks[1:]
        near = value + partner(value, *first)
        if masks:
            second, masks = masks[0], masks[1:]
            both = (first[0] ^ second[0], first[1] ^ second[1])
            near = near + (partner(value, *second) + partner(value, *both))
        value = near
    return value


def in_two(value):
    high = value.astype(BF16)
    return high, (value - high.astype(F32)).astype(BF16)


def tiles(value):
    rows, columns = value.shape
    return [
        [value[r : r + SUBLANES, c : min(c + LANES, columns)] for c in range(0, columns, LANES)]
        for r in range(0, rows, SUBLANES)
    ]


def joined(groups):
    return jnp.concatenate([jnp.concatenate(group, axis=1) for group in groups], axis=0)


def eliminated(gram, extra):
    gram = [list(group) for group in gram]
    extra = [list(group) for group in extra]
    row_id = lax.broadcasted_iota(jnp.int32, (SUBLANES, LANES), 0)

    def row(tile, r):
        return jnp.broadcast_to(tile[r : r + 1, :], tile.shape)

    def column(tile, c):
        return jnp.broadcast_to(tile[:, c : c + 1], (SUBLANES, LANES))

    def spread(tile, r):
        return jnp.take_along_axis(tile, jnp.full(tile.shape, r, jnp.int32), axis=0)

    def less(tile, factor, other):
        return tile - factor[:, : tile.shape[1]] * other

    for g in range(len(gram)):
        at, first = divmod(g * SUBLANES, LANES)
        both = [gram[h] + extra[h] for h in range(len(gram))]
        rows = [[row(t, q) for t in both[g]] for q in range(SUBLANES)]
        pivots = [column(gram[g][at], first + b) for b in range(SUBLANES)]
        block = [[spread(pivots[b], a) if b >= a else None for b in range(SUBLANES)] for a in range(SUBLANES)]
        below = range(g + 1, len(gram))
        columns = {h: [column(gram[h][at], first + q) for q in range(SUBLANES)] for h in below}
        scales, inverses = [], []
        for q in range(SUBLANES):
            scales.append(lax.rsqrt(block[q][q]))
            inverses.append(scales[q] * scales[q])
            for b in range(q + 1, SUBLANES):
                factor = block[q][b] * inverses[q]
                for c in range(b, SUBLANES):
                    block[b][c] = block[b][c] - factor * block[q][c]
                rows[b] = [less(t, factor, r) for t, r in zip(rows[b], rows[q])]
                for h in below:
                    columns[h][b] = columns[h][b] - factor * columns[h][q]
        for h in below:
            for q in range(SUBLANES):
                factor = columns[h][q] * inverses[q]
                both[h] = [less(t, factor, r) for t, r in zip(both[h], rows[q])]
        for q in range(SUBLANES):
            both[g] = [
                jnp.where((row_id == q)[:, : t.shape[1]], r * scales[q][:, : t.shape[1]], t)
                for t, r in zip(both[g], rows[q])
            ]
        for h in range(g, len(gram)):
            gram[h], extra[h] = both[h][: len(gram[h])], both[h][len(gram[h]) :]
    return gram, extra


def orth_pass(rows, *more):
    inner_gram = lax.dot_general(rows, rows, ROWS_BY_ROWS, precision=precise, preferred_element_type=F32)
    widths = [v.shape[1] for v in (rows, *more)]
    extra = [sum(parts, []) for parts in zip(*(tiles(v) for v in (rows, *more)))]
    groups = eliminated(tiles(inner_gram), extra)[1]
    out, at = [], 0
    for width in widths:
        count = -(-width // LANES)
        out.append(joined([group[at : at + count] for group in groups]))
        at += count
    return out


def triangle_ids(n):
    return lax.broadcasted_iota(jnp.int32, (n, n), 0), lax.broadcasted_iota(jnp.int32, (n, n), 1)


def folded(full):
    half = full.shape[0] // 2
    r, c = triangle_ids(half)
    corner = full[half:, half:]
    diagonal = jnp.sum(jnp.where(r == c, corner, 0.0), axis=0, keepdims=True)
    return jnp.where(r > c, corner, full[:half, :half]), full[:half, half:], diagonal


def opened(fold, upper, diagonal):
    half = fold.shape[0]
    r, c = triangle_ids(half)
    turned = fold.T
    first = jnp.where(c >= r, fold, turned)
    second = jnp.where(r > c, fold, jnp.where(r == c, jnp.broadcast_to(diagonal, fold.shape), turned))
    return jnp.concatenate(
        [jnp.concatenate([first, upper], axis=1), jnp.concatenate([upper.T, second], axis=1)], axis=0
    )


def species_weights(rows, repeat):
    high, low = in_two(jnp.concatenate([rows] * repeat, axis=0).T)
    weights = jnp.concatenate([high, low], axis=1)
    return jnp.concatenate([weights, weights], axis=0)


def times(value, weights):
    out = jnp.dot(jnp.concatenate(in_two(value), axis=1), weights, preferred_element_type=F32)
    half = out.shape[1] // 2
    return out[:, :half] + out[:, half:]


def packed(narrow, first, count, stride, rank):
    lane = lax.broadcasted_iota(jnp.int32, (count, LANES), 1)
    pack = LANES // rank
    out = narrow[pl.ds(first + pack - 1, count, stride=stride), :]
    for q in range(pack - 2, -1, -1):
        out = jnp.where(lane < (q + 1) * rank, narrow[pl.ds(first + q, count, stride=stride), :], out)
    return out


def gram_kernel(cuts, place, field, mine, other, held, arrived):
    copies = [
        pltpu.make_async_copy(field.at[a:b], held.at[a:b], arrived.at[i])
        for i, (a, b) in enumerate(zip(cuts[:-1], cuts[1:]))
    ]
    for copy in copies:
        copy.start()
    square = cross = 0.0
    for copy, a, b in zip(copies, cuts[:-1], cuts[1:]):
        copy.wait()
        high, low = in_two(held[a:b])
        square = square + lax.dot_general(high, high, COLUMNS_BY_COLUMNS, preferred_element_type=F32)
        cross = cross + lax.dot_general(high, low, COLUMNS_BY_COLUMNS, preferred_element_type=F32)
    fold, upper, diagonal = folded(square + (cross + cross.T))
    half = fold.shape[0]
    edge = SUBLANES
    even = place[0] & 1 == 0

    def put(first, second):
        first[:half] = fold
        first[half:] = upper[:edge]
        second[: half - edge] = upper[edge:]
        second[half - edge :] = jnp.broadcast_to(diagonal, (2 * edge, half))

    @pl.when(even)
    def _():
        put(mine, other)

    @pl.when(jnp.logical_not(even))
    def _():
        put(other, mine)


def local_gram(place, unfolded):
    rows, z = unfolded.shape
    cuts = [0, rows // 8, rows // 2, rows]
    out = jax.ShapeDtypeStruct((z // 2 + SUBLANES, z // 2), F32)
    return pl.pallas_call(
        functools.partial(gram_kernel, cuts),
        out_shape=[out, out, jax.ShapeDtypeStruct((rows, z), F32)],
        in_specs=[SMEM, HBM],
        out_specs=[VMEM] * 3,
        scratch_shapes=[pltpu.SemaphoreType.DMA((len(cuts) - 1,))],
        compiler_params=pltpu.CompilerParams(vmem_limit_bytes=32 << 20),
        name="gram",
    )(place, unfolded)


def begin_kernel(place, mine, other, start, basis, image, gram):
    half = mine.shape[1]
    edge = SUBLANES
    even = place[0] & 1 == 0
    first = jnp.where(even, mine[...], other[...])
    second = jnp.where(even, other[...], mine[...])
    gram[...] = opened(
        first[:half],
        jnp.concatenate([first[half:], second[: half - edge]], axis=0),
        second[half - edge : half - edge + 1],
    )
    basis[...] = start[...]

    def multiplied():
        return jnp.dot(basis[...], gram[...], precision=precise, preferred_element_type=F32)

    @pl.loop(0, ITERS - 2)
    def _(iteration):
        basis[...] = orth_pass(*orth_pass(multiplied()))[0]

    basis[...] = orth_pass(multiplied())[0]
    image[...] = multiplied()


def begin(place, mine, other, start_rows):
    z = start_rows.shape[1]
    rows = jax.ShapeDtypeStruct(start_rows.shape, F32)
    return pl.pallas_call(
        begin_kernel,
        out_shape=[rows, rows, jax.ShapeDtypeStruct((z, z), F32)],
        in_specs=[SMEM] + [VMEM] * 3,
        out_specs=[VMEM] * 3,
        compiler_params=SMALL,
        name="begin",
    )(place, mine, other, start_rows)


def finish_kernel(basis, gram, out, factor):
    rank = basis.shape[0]
    r, c = triangle_ids(rank)
    rows, turn = orth_pass(basis[...], jnp.where(r == c, 1.0, 0.0))
    rows = jnp.dot(rows, gram[...], precision=precise, preferred_element_type=F32)
    for _ in range(2):
        rows, turn = orth_pass(rows, turn)
    out[...] = rows
    factor[...] = turn


def finish(basis, gram):
    rank, z = basis.shape
    return pl.pallas_call(
        finish_kernel,
        out_shape=[jax.ShapeDtypeStruct((rank, z), F32), jax.ShapeDtypeStruct((rank, rank), F32)],
        in_specs=[VMEM] * 2,
        out_specs=[VMEM] * 2,
        compiler_params=SMALL,
        cost_estimate=pl.CostEstimate(flops=1 << 30, bytes_accessed=1 << 24, transcendentals=0),
        name="finish",
    )(basis, gram)


def ahead_kernel(d, species, place, field, image, out, narrow):
    share, x_cells, width = out.shape
    rank = image.shape[0]
    across = share * species
    start = pl.multiple_of((place[0] ^ d) * across, across)
    cells = field[:, pl.ds(start, across), :]
    narrow[...] = times(cells.reshape(x_cells * across, cells.shape[2]), species_weights(image[...], LANES // rank))
    for y in range(share):
        for t in range(width // LANES):
            out[y, :, t * LANES : (t + 1) * LANES] = packed(
                narrow, y * species + t * (LANES // rank), x_cells, across, rank
            )


def contract_ahead(place, field, image, x_cells, y_cells, species, x_parts, d):
    z = field.shape[1]
    rank = image.shape[0]
    share = y_cells // x_parts
    return pl.pallas_call(
        functools.partial(ahead_kernel, d, species),
        out_shape=jax.ShapeDtypeStruct((share, x_cells, species * rank), F32),
        in_specs=[SMEM, VMEM, VMEM],
        out_specs=VMEM,
        scratch_shapes=[pltpu.VMEM((x_cells * share * species, LANES), F32)],
        compiler_params=SMALL,
        cost_estimate=pl.CostEstimate(flops=1 << 30, bytes_accessed=1 << 22, transcendentals=0),
    )(place, field.reshape(x_cells, y_cells * species, z), image)


def core_kernel(species, y_cells, place, field, basis, core, *refs):
    outs, (weights, narrow, strip) = refs[:-3], refs[-3:]
    share, step, width = outs[0].shape
    rank = basis.shape[0]
    cells = core.shape[0]
    half = len(outs)
    near = place[0] // half * half

    @pl.when(pl.program_id(0) == 0)
    def _():
        weights[...] = species_weights(basis[...], LANES // rank)

    block = narrow.shape[0]
    narrow[...] = times(field[pl.ds(pl.multiple_of(pl.program_id(0) * block, block), block), :], weights[...])
    for t in range(width // LANES):
        lanes = slice(t * LANES, (t + 1) * LANES)
        strip[...] = packed(narrow, t * (LANES // rank), cells, species, rank)
        core[:, lanes] = strip[...]
        for d, out in enumerate(outs):
            part = near + ((place[0] ^ d) & (half - 1))
            for y in range(share):
                out[y, :, lanes] = strip[pl.ds(part * share + y, step, stride=y_cells), :]


def contract(place, unfolded, basis, x_cells, y_cells, species, x_parts):
    rows, z = unfolded.shape
    rank = basis.shape[0]
    steps = 4
    block, cells = rows // steps, rows // species // steps
    width = species * rank
    share = y_cells // x_parts
    pieces = x_parts // 2
    return pl.pallas_call(
        functools.partial(core_kernel, species, y_cells),
        grid=(steps,),
        out_shape=[jax.ShapeDtypeStruct((rows // species, width), F32)]
        + [jax.ShapeDtypeStruct((share, x_cells, width), F32)] * pieces,
        in_specs=[
            SMEM,
            VMEM,
            pl.BlockSpec((rank, z), lambda i: (0, 0)),
        ],
        out_specs=[pl.BlockSpec((cells, width), lambda i: (i, 0))]
        + [pl.BlockSpec((share, x_cells // steps, width), lambda i: (0, i, 0))] * pieces,
        scratch_shapes=[
            pltpu.VMEM((2 * z, 2 * LANES), BF16),
            pltpu.VMEM((block, LANES), F32),
            pltpu.VMEM((cells, LANES), F32),
        ],
        compiler_params=SMALL,
        cost_estimate=pl.CostEstimate(flops=1 << 31, bytes_accessed=1 << 24, transcendentals=0),
        name="core",
    )(place, unfolded, basis)


def product_kernel(place, factor, *refs):
    pieces, (out, turn) = refs[:-2], refs[-2:]
    share, size, width = pieces[0].shape
    rank = factor.shape[0]
    near, far = pieces[: len(pieces) // 2], pieces[len(pieces) // 2 :]
    turn[...] = jnp.zeros_like(turn)
    for part, value in enumerate(in_two(factor[...])):
        for side in range(2):
            for q in range(LANES // rank):
                turn[
                    part * LANES + q * rank : part * LANES + (q + 1) * rank,
                    side * LANES + q * rank : side * LANES + (q + 1) * rank,
                ] = value
    strips = [
        piece[y, :, t : t + LANES] for piece in far for y in range(share) for t in range(0, width, LANES)
    ]
    both = jnp.concatenate(in_two(jnp.concatenate(strips, axis=0)), axis=1)
    turned = lax.dot_general(both, turn[...], ROWS_BY_ROWS, preferred_element_type=F32)
    turned = turned[:, :LANES] + turned[:, LANES:]
    count = width // LANES
    square = cross = 0.0
    for y in range(share):
        rows = [piece[y] for piece in near]
        for d in range(len(far)):
            at = (d * share + y) * count
            rows.append(
                jnp.concatenate([turned[(at + t) * size : (at + t + 1) * size] for t in range(count)], axis=1)
            )
        high, low = in_two(jnp.concatenate(rows, axis=0))
        square = square + lax.dot_general(high, high, ROWS_BY_ROWS, preferred_element_type=F32)
        cross = cross + lax.dot_general(high, low, ROWS_BY_ROWS, preferred_element_type=F32)
    total = square + (cross + cross.T)
    for bit in bits(len(pieces)):
        step = size * bit
        swap = place[0] & bit != 0
        for axis in (0, 1):
            parts = [lax.slice_in_dim(total, c, c + step, axis=axis) for c in range(0, total.shape[axis], step)]
            swapped = jnp.concatenate([parts[c ^ 1] for c in range(len(parts))], axis=axis)
            total = jnp.where(swap, swapped, total)
    fold, upper, diagonal = folded(total)
    half = fold.shape[0]
    out[:half] = jnp.concatenate([fold, upper], axis=1)
    out[half:] = jnp.broadcast_to(jnp.concatenate([diagonal, diagonal], axis=1), (SUBLANES, 2 * half))


def product(place, factor, pieces):
    n = len(pieces) * pieces[0].shape[1]
    return pl.pallas_call(
        product_kernel,
        out_shape=jax.ShapeDtypeStruct((n // 2 + SUBLANES, n), F32),
        in_specs=[SMEM] + [VMEM] * (len(pieces) + 1),
        out_specs=VMEM,
        scratch_shapes=[pltpu.VMEM((2 * LANES, 2 * LANES), BF16)],
        compiler_params=SMALL,
        name="product",
    )(place, factor, *pieces)


def triangle_kernel(scale, gram, out):
    half = gram.shape[1] // 2
    full = opened(gram[:half, :half], gram[:half, half:], gram[half : half + 1, :half])
    upper = joined(eliminated(tiles(full), [[] for _ in range(0, 2 * half, SUBLANES)])[0])
    r, c = triangle_ids(2 * half)
    out[...] = jnp.where(c >= r, upper * scale, 0.0)


def triangle(gram, scale):
    n = gram.shape[1]
    return pl.pallas_call(
        functools.partial(triangle_kernel, scale),
        out_shape=jax.ShapeDtypeStruct((n, n), F32),
        in_specs=[VMEM],
        out_specs=VMEM,
        compiler_params=SMALL,
        name="triangle",
    )(gram)


def local(state_field, start_basis):
    x_cells, y_cells, species, z_cells = state_field.shape
    rank_kept = start_basis.shape[1]
    unfolded = state_field.reshape(x_cells * y_cells * species, z_cells)
    x_parts = lax.axis_size("gx")
    place = lax.axis_index("gx").astype(jnp.int32).reshape(1)
    mine, other, held = local_gram(place, pltpu.with_memory_space_constraint(unfolded, pltpu.HBM))
    mine = summed(mine + partner(other, 1))
    other = partner(mine, 1)
    basis, image, gram = begin(place, mine, other, start_basis.T)
    far = []
    for d in range(x_parts // 2, x_parts):
        piece = contract_ahead(place, held, image, x_cells, y_cells, species, x_parts, d)
        far.append(partner(piece, d))
    basis_rows, factor = finish(basis, gram)
    core_tensor, *near = contract(place, held, basis_rows, x_cells, y_cells, species, x_parts)
    near = [partner(piece, d) if d else piece for d, piece in enumerate(near)]
    gram_x = product(place, factor, near + far)
    gram_x = summed(gram_x + partner(gram_x, 1))
    column_count = y_cells * lax.axis_size("gy") * species * rank_kept
    x_triangle = triangle(gram_x, 1.0 / column_count**0.5)
    return (core_tensor.reshape(x_cells, y_cells, species * rank_kept), basis_rows.T, x_triangle)


def solution(mesh):
    return jax.shard_map(
        local,
        mesh=mesh,
        in_specs=(P("gx", "gy", None, None), P()),
        out_specs=(P("gx", "gy", None), P(), P()),
        check_vma=False,
    )
```

```python
import functools

import jax
import jax.numpy as jnp
from jax import lax
from jax.experimental import pallas as pl
from jax.experimental.pallas import tpu as pltpu
from jax.sharding import PartitionSpec as P


ITERS = 3
F32, BF16 = jnp.float32, jnp.bfloat16
LANES, SUBLANES = 128, 8

precise = lax.Precision.HIGHEST
ROWS_BY_ROWS = (((1,), (1,)), ((), ()))
COLUMNS_BY_COLUMNS = (((0,), (0,)), ((), ()))
VMEM = pl.BlockSpec(memory_space=pltpu.VMEM)
SMEM = pl.BlockSpec(memory_space=pltpu.SMEM)
HBM = pl.BlockSpec(memory_space=pltpu.HBM)
SMALL = pltpu.CompilerParams(vmem_limit_bytes=32 << 20)


def bits(size):
    return [1 << b for b in range(size.bit_length() - 1)]


def partner(value, x_mask, y_mask=0):
    x_size, y_size = lax.axis_size("gx"), lax.axis_size("gy")
    pairs = [
        (x * y_size + y, (x ^ x_mask) * y_size + (y ^ y_mask)) for x in range(x_size) for y in range(y_size)
    ]
    return lax.ppermute(value, ("gx", "gy"), pairs)


def summed(value):
    masks = [(bit, 0) for bit in bits(lax.axis_size("gx"))[1:]] + [(0, bit) for bit in bits(lax.axis_size("gy"))]
    while masks:
        first, masks = masks[0], masks[1:]
        near = value + partner(value, *first)
        if masks:
            second, masks = masks[0], masks[1:]
            both = (first[0] ^ second[0], first[1] ^ second[1])
            near = near + (partner(value, *second) + partner(value, *both))
        value = near
    return value


def in_two(value):
    high = value.astype(BF16)
    return high, (value - high.astype(F32)).astype(BF16)


def tiles(value):
    rows, columns = value.shape
    return [
        [value[r : r + SUBLANES, c : min(c + LANES, columns)] for c in range(0, columns, LANES)]
        for r in range(0, rows, SUBLANES)
    ]


def joined(groups):
    return jnp.concatenate([jnp.concatenate(group, axis=1) for group in groups], axis=0)


def eliminated(gram, extra):
    gram = [list(group) for group in gram]
    extra = [list(group) for group in extra]
    row_id = lax.broadcasted_iota(jnp.int32, (SUBLANES, LANES), 0)

    def row(tile, r):
        return jnp.broadcast_to(tile[r : r + 1, :], tile.shape)

    def column(tile, c):
        return jnp.broadcast_to(tile[:, c : c + 1], (SUBLANES, LANES))

    def spread(tile, r):
        return jnp.take_along_axis(tile, jnp.full(tile.shape, r, jnp.int32), axis=0)

    def less(tile, factor, other):
        return tile - factor[:, : tile.shape[1]] * other

    for g in range(len(gram)):
        at, first = divmod(g * SUBLANES, LANES)
        both = [gram[h] + extra[h] for h in range(len(gram))]
        rows = [[row(t, q) for t in both[g]] for q in range(SUBLANES)]
        pivots = [column(gram[g][at], first + b) for b in range(SUBLANES)]
        block = [[spread(pivots[b], a) if b >= a else None for b in range(SUBLANES)] for a in range(SUBLANES)]
        below = range(g + 1, len(gram))
        columns = {h: [column(gram[h][at], first + q) for q in range(SUBLANES)] for h in below}
        scales, inverses = [], []
        for q in range(SUBLANES):
            scales.append(lax.rsqrt(block[q][q]))
            inverses.append(scales[q] * scales[q])
            for b in range(q + 1, SUBLANES):
                factor = block[q][b] * inverses[q]
                for c in range(b, SUBLANES):
                    block[b][c] = block[b][c] - factor * block[q][c]
                rows[b] = [less(t, factor, r) for t, r in zip(rows[b], rows[q])]
                for h in below:
                    columns[h][b] = columns[h][b] - factor * columns[h][q]
        for h in below:
            for q in range(SUBLANES):
                factor = columns[h][q] * inverses[q]
                both[h] = [less(t, factor, r) for t, r in zip(both[h], rows[q])]
        for q in range(SUBLANES):
            both[g] = [
                jnp.where((row_id == q)[:, : t.shape[1]], r * scales[q][:, : t.shape[1]], t)
                for t, r in zip(both[g], rows[q])
            ]
        for h in range(g, len(gram)):
            gram[h], extra[h] = both[h][: len(gram[h])], both[h][len(gram[h]) :]
    return gram, extra


def orth_pass(rows, *more):
    inner_gram = lax.dot_general(rows, rows, ROWS_BY_ROWS, precision=precise, preferred_element_type=F32)
    widths = [v.shape[1] for v in (rows, *more)]
    extra = [sum(parts, []) for parts in zip(*(tiles(v) for v in (rows, *more)))]
    groups = eliminated(tiles(inner_gram), extra)[1]
    out, at = [], 0
    for width in widths:
        count = -(-width // LANES)
        out.append(joined([group[at : at + count] for group in groups]))
        at += count
    return out


def triangle_ids(n):
    return lax.broadcasted_iota(jnp.int32, (n, n), 0), lax.broadcasted_iota(jnp.int32, (n, n), 1)


def folded(full):
    half = full.shape[0] // 2
    r, c = triangle_ids(half)
    corner = full[half:, half:]
    diagonal = jnp.sum(jnp.where(r == c, corner, 0.0), axis=0, keepdims=True)
    return jnp.where(r > c, corner, full[:half, :half]), full[:half, half:], diagonal


def opened(fold, upper, diagonal):
    half = fold.shape[0]
    r, c = triangle_ids(half)
    turned = fold.T
    first = jnp.where(c >= r, fold, turned)
    second = jnp.where(r > c, fold, jnp.where(r == c, jnp.broadcast_to(diagonal, fold.shape), turned))
    return jnp.concatenate(
        [jnp.concatenate([first, upper], axis=1), jnp.concatenate([upper.T, second], axis=1)], axis=0
    )


def species_weights(rows, repeat):
    high, low = in_two(jnp.concatenate([rows] * repeat, axis=0).T)
    weights = jnp.concatenate([high, low], axis=1)
    return jnp.concatenate([weights, weights], axis=0)


def times(value, weights):
    out = jnp.dot(jnp.concatenate(in_two(value), axis=1), weights, preferred_element_type=F32)
    half = out.shape[1] // 2
    return out[:, :half] + out[:, half:]


def packed(narrow, first, count, stride, rank):
    lane = lax.broadcasted_iota(jnp.int32, (count, LANES), 1)
    pack = LANES // rank
    out = narrow[pl.ds(first + pack - 1, count, stride=stride), :]
    for q in range(pack - 2, -1, -1):
        out = jnp.where(lane < (q + 1) * rank, narrow[pl.ds(first + q, count, stride=stride), :], out)
    return out


def gram_kernel(cuts, place, field, mine, other, held, arrived):
    copies = [
        pltpu.make_async_copy(field.at[a:b], held.at[a:b], arrived.at[i])
        for i, (a, b) in enumerate(zip(cuts[:-1], cuts[1:]))
    ]
    for copy in copies:
        copy.start()
    square = cross = 0.0
    for copy, a, b in zip(copies, cuts[:-1], cuts[1:]):
        copy.wait()
        high, low = in_two(held[a:b])
        square = square + lax.dot_general(high, high, COLUMNS_BY_COLUMNS, preferred_element_type=F32)
        cross = cross + lax.dot_general(high, low, COLUMNS_BY_COLUMNS, preferred_element_type=F32)
    fold, upper, diagonal = folded(square + (cross + cross.T))
    half = fold.shape[0]
    edge = SUBLANES
    even = place[0] & 1 == 0

    def put(first, second):
        first[:half] = fold
        first[half:] = upper[:edge]
        second[: half - edge] = upper[edge:]
        second[half - edge :] = jnp.broadcast_to(diagonal, (2 * edge, half))

    @pl.when(even)
    def _():
        put(mine, other)

    @pl.when(jnp.logical_not(even))
    def _():
        put(other, mine)


def local_gram(place, unfolded):
    rows, z = unfolded.shape
    cuts = [0, rows // 8, rows // 2, rows]
    out = jax.ShapeDtypeStruct((z // 2 + SUBLANES, z // 2), F32)
    return pl.pallas_call(
        functools.partial(gram_kernel, cuts),
        out_shape=[out, out, jax.ShapeDtypeStruct((rows, z), F32)],
        in_specs=[SMEM, HBM],
        out_specs=[VMEM] * 3,
        scratch_shapes=[pltpu.SemaphoreType.DMA((len(cuts) - 1,))],
        compiler_params=pltpu.CompilerParams(vmem_limit_bytes=32 << 20),
        name="gram",
    )(place, unfolded)


def begin_kernel(place, mine, other, start, basis, image, gram):
    half = mine.shape[1]
    edge = SUBLANES
    even = place[0] & 1 == 0
    first = jnp.where(even, mine[...], other[...])
    second = jnp.where(even, other[...], mine[...])
    gram[...] = opened(
        first[:half],
        jnp.concatenate([first[half:], second[: half - edge]], axis=0),
        second[half - edge : half - edge + 1],
    )
    basis[...] = start[...]

    def multiplied():
        return jnp.dot(basis[...], gram[...], precision=precise, preferred_element_type=F32)

    @pl.loop(0, ITERS - 2)
    def _(iteration):
        basis[...] = orth_pass(*orth_pass(multiplied()))[0]

    basis[...] = orth_pass(multiplied())[0]
    image[...] = multiplied()


def begin(place, mine, other, start_rows):
    z = start_rows.shape[1]
    rows = jax.ShapeDtypeStruct(start_rows.shape, F32)
    return pl.pallas_call(
        begin_kernel,
        out_shape=[rows, rows, jax.ShapeDtypeStruct((z, z), F32)],
        in_specs=[SMEM] + [VMEM] * 3,
        out_specs=[VMEM] * 3,
        compiler_params=SMALL,
        name="begin",
    )(place, mine, other, start_rows)


def finish_kernel(basis, gram, out, again, factor):
    rank = basis.shape[0]
    r, c = triangle_ids(rank)
    rows, turn = orth_pass(basis[...], jnp.where(r == c, 1.0, 0.0))
    rows = jnp.dot(rows, gram[...], precision=precise, preferred_element_type=F32)
    for _ in range(2):
        rows, turn = orth_pass(rows, turn)
    out[...] = rows
    again[...] = rows
    factor[...] = turn


def finish(basis, gram):
    rank, z = basis.shape
    return pl.pallas_call(
        finish_kernel,
        out_shape=[jax.ShapeDtypeStruct((rank, z), F32)] * 2 + [jax.ShapeDtypeStruct((rank, rank), F32)],
        in_specs=[VMEM] * 2,
        out_specs=[VMEM] * 3,
        compiler_params=SMALL,
        cost_estimate=pl.CostEstimate(flops=1 << 30, bytes_accessed=1 << 24, transcendentals=0),
        name="finish",
    )(basis, gram)


def ahead_kernel(d, share, skip, species, place, field, image, out, narrow):
    count, x_cells, width = out.shape
    rank = image.shape[0]
    across = count * species
    start = pl.multiple_of(((place[0] ^ d) * share + skip) * species, species)
    cells = field[:, pl.ds(start, across), :]
    narrow[...] = times(cells.reshape(x_cells * across, cells.shape[2]), species_weights(image[...], LANES // rank))
    for y in range(count):
        for t in range(width // LANES):
            out[y, :, t * LANES : (t + 1) * LANES] = packed(
                narrow, y * species + t * (LANES // rank), x_cells, across, rank
            )


def contract_ahead(place, field, image, x_cells, y_cells, species, share, d, skip, count):
    z = field.shape[1]
    rank = image.shape[0]
    return pl.pallas_call(
        functools.partial(ahead_kernel, d, share, skip, species),
        out_shape=jax.ShapeDtypeStruct((count, x_cells, species * rank), F32),
        in_specs=[SMEM, VMEM, VMEM],
        out_specs=VMEM,
        scratch_shapes=[pltpu.VMEM((x_cells * count * species, LANES), F32)],
        compiler_params=SMALL,
        cost_estimate=pl.CostEstimate(flops=1 << 30, bytes_accessed=1 << 22, transcendentals=0),
    )(place, field.reshape(x_cells, y_cells * species, z), image)


def core_kernel(species, far, place, field, basis, *refs):
    refs = refs[1:] if far else refs
    core, outs, (weights, narrow, strip) = refs[0], refs[1:-3], refs[-3:]
    step, across, width = core.shape
    rank, z = basis.shape
    cells = step * across
    rows = across * species
    start = pl.multiple_of(far_or_near(place, far) * rows, rows)

    @pl.when(pl.program_id(0) == 0)
    def _():
        weights[...] = species_weights(basis[...], LANES // rank)

    block = field[pl.ds(pl.program_id(0) * step, step), pl.ds(start, rows), :]
    narrow[...] = times(block.reshape(step * rows, z), weights[...])
    for t in range(width // LANES):
        lanes = slice(t * LANES, (t + 1) * LANES)
        strip[...] = packed(narrow, t * (LANES // rank), cells, species, rank)
        core[:, :, lanes] = strip[...].reshape(step, across, LANES)
        for d, out in enumerate(outs):
            share = out.shape[0]
            first = ((place[0] ^ d) & (len(outs) - 1)) * share
            for y in range(share):
                out[y, :, lanes] = strip[pl.ds(first + y, step, stride=across), :]


def far_or_near(place, far):
    return 1 - place[1] if far else place[1]


def contract(place, field, basis, x_cells, y_cells, species, x_parts, core=None):
    z = field.shape[1]
    rank = basis.shape[0]
    steps = 4
    step, across = x_cells // steps, y_cells // 2
    width = species * rank
    share = y_cells // x_parts
    far = core is not None
    pieces = 0 if far else x_parts // 2
    return pl.pallas_call(
        functools.partial(core_kernel, species, far),
        grid_spec=pltpu.PrefetchScalarGridSpec(
            num_scalar_prefetch=1,
            grid=(steps,),
            in_specs=[VMEM, pl.BlockSpec((rank, z), lambda i, place: (0, 0))]
            + ([pl.BlockSpec(memory_space=pl.ANY)] if far else []),
            out_specs=[pl.BlockSpec((step, across, width), lambda i, place: (i, far_or_near(place, far), 0))]
            + [pl.BlockSpec((share, step, width), lambda i, place: (0, i, 0))] * pieces,
            scratch_shapes=[
                pltpu.VMEM((2 * z, 2 * LANES), BF16),
                pltpu.VMEM((step * across * species, LANES), F32),
                pltpu.VMEM((step * across, LANES), F32),
            ],
        ),
        out_shape=[jax.ShapeDtypeStruct((x_cells, y_cells, width), F32)]
        + [jax.ShapeDtypeStruct((share, x_cells, width), F32)] * pieces,
        input_output_aliases={3: 0} if far else {},
        compiler_params=SMALL,
        cost_estimate=pl.CostEstimate(flops=1 << 30, bytes_accessed=1 << 23, transcendentals=0),
        name="far_core" if far else "near_core",
    )(place, field.reshape(x_cells, y_cells * species, z), basis, *([core] if far else []))


def product_kernel(near_count, place, factor, *refs):
    near, far, (out, turn) = refs[:near_count], refs[near_count:-2], refs[-2:]
    share, size, width = near[0].shape
    rank = factor.shape[0]
    turn[...] = jnp.zeros_like(turn)
    for part, value in enumerate(in_two(factor[...])):
        for side in range(2):
            for q in range(LANES // rank):
                turn[
                    part * LANES + q * rank : part * LANES + (q + 1) * rank,
                    side * LANES + q * rank : side * LANES + (q + 1) * rank,
                ] = value
    strips = [
        piece[y, :, t : t + LANES]
        for piece in far
        for y in range(piece.shape[0])
        for t in range(0, width, LANES)
    ]
    both = jnp.concatenate(in_two(jnp.concatenate(strips, axis=0)), axis=1)
    turned = lax.dot_general(both, turn[...], ROWS_BY_ROWS, preferred_element_type=F32)
    turned = turned[:, :LANES] + turned[:, LANES:]
    count = width // LANES
    square = cross = 0.0
    for y in range(share):
        rows = [piece[y] for piece in near]
        for d in range(near_count):
            at = (d * share + y) * count
            rows.append(
                jnp.concatenate([turned[(at + t) * size : (at + t + 1) * size] for t in range(count)], axis=1)
            )
        high, low = in_two(jnp.concatenate(rows, axis=0))
        square = square + lax.dot_general(high, high, ROWS_BY_ROWS, preferred_element_type=F32)
        cross = cross + lax.dot_general(high, low, ROWS_BY_ROWS, preferred_element_type=F32)
    total = square + (cross + cross.T)
    for bit in bits(2 * near_count):
        step = size * bit
        swap = place[0] & bit != 0
        for axis in (0, 1):
            parts = [lax.slice_in_dim(total, c, c + step, axis=axis) for c in range(0, total.shape[axis], step)]
            swapped = jnp.concatenate([parts[c ^ 1] for c in range(len(parts))], axis=axis)
            total = jnp.where(swap, swapped, total)
    fold, upper, diagonal = folded(total)
    half = fold.shape[0]
    out[:half] = jnp.concatenate([fold, upper], axis=1)
    out[half:] = jnp.broadcast_to(jnp.concatenate([diagonal, diagonal], axis=1), (SUBLANES, 2 * half))


def product(place, factor, near, far):
    n = 2 * len(near) * near[0].shape[1]
    return pl.pallas_call(
        functools.partial(product_kernel, len(near)),
        out_shape=jax.ShapeDtypeStruct((n // 2 + SUBLANES, n), F32),
        in_specs=[SMEM] + [VMEM] * (1 + len(near) + len(far)),
        out_specs=VMEM,
        scratch_shapes=[pltpu.VMEM((2 * LANES, 2 * LANES), BF16)],
        compiler_params=SMALL,
        name="product",
    )(place, factor, *near, *far)


def triangle_kernel(scale, gram, out):
    half = gram.shape[1] // 2
    full = opened(gram[:half, :half], gram[:half, half:], gram[half : half + 1, :half])
    upper = joined(eliminated(tiles(full), [[] for _ in range(0, 2 * half, SUBLANES)])[0])
    r, c = triangle_ids(2 * half)
    out[...] = jnp.where(c >= r, upper * scale, 0.0)


def triangle(gram, scale):
    n = gram.shape[1]
    return pl.pallas_call(
        functools.partial(triangle_kernel, scale),
        out_shape=jax.ShapeDtypeStruct((n, n), F32),
        in_specs=[VMEM],
        out_specs=VMEM,
        compiler_params=SMALL,
        name="triangle",
    )(gram)


def local(state_field, start_basis):
    x_cells, y_cells, species, z_cells = state_field.shape
    rank_kept = start_basis.shape[1]
    unfolded = state_field.reshape(x_cells * y_cells * species, z_cells)
    x_parts = lax.axis_size("gx")
    place = lax.axis_index("gx").astype(jnp.int32).reshape(1)
    mine, other, held = local_gram(place, pltpu.with_memory_space_constraint(unfolded, pltpu.HBM))
    mine = summed(mine + partner(other, 1))
    other = partner(mine, 1)
    basis, image, gram = begin(place, mine, other, start_basis.T)
    far = []
    share = y_cells // x_parts
    for d, skip, count in far_pieces(x_parts, share):
        piece = contract_ahead(place, held, image, x_cells, y_cells, species, share, d, skip, count)
        far.append(partner(piece, d))
    basis_rows, basis, factor = finish(basis, gram)
    halves = jnp.concatenate([place, place // (x_parts // 2)])
    core_tensor, *near = contract(halves, held, basis, x_cells, y_cells, species, x_parts)
    near = [partner(piece, d) if d else piece for d, piece in enumerate(near)]
    (core_tensor,) = contract(halves, held, basis, x_cells, y_cells, species, x_parts, core_tensor)
    gram_x = product(place, factor, near, far)
    gram_x = summed(gram_x + partner(gram_x, 1))
    column_count = y_cells * lax.axis_size("gy") * species * rank_kept
    x_triangle = triangle(gram_x, 1.0 / column_count**0.5)
    return (core_tensor, basis_rows.T, x_triangle)


def far_pieces(x_parts, share):
    whole = [(d, 0, share) for d in range(x_parts // 2, x_parts)]
    d, first = whole[0][0], share // 2
    return ([(d, 0, first), (d, first, share - first)] if first else whole[:1]) + whole[1:]


def solution(mesh):
    return jax.shard_map(
        local,
        mesh=mesh,
        in_specs=(P("gx", "gy", None, None), P()),
        out_specs=(P("gx", "gy", None), P(), P()),
        check_vma=False,
    )
```

```python
import functools

import jax
import jax.numpy as jnp
from jax import lax
from jax.experimental import pallas as pl
from jax.experimental.pallas import tpu as pltpu
from jax.sharding import PartitionSpec as P


ITERS = 3
F32, BF16 = jnp.float32, jnp.bfloat16
LANES, SUBLANES = 128, 8

precise = lax.Precision.HIGHEST
ROWS_BY_ROWS = (((1,), (1,)), ((), ()))
COLUMNS_BY_COLUMNS = (((0,), (0,)), ((), ()))
VMEM = pl.BlockSpec(memory_space=pltpu.VMEM)
SMEM = pl.BlockSpec(memory_space=pltpu.SMEM)
HBM = pl.BlockSpec(memory_space=pltpu.HBM)
SMALL = pltpu.CompilerParams(vmem_limit_bytes=32 << 20)


def bits(size):
    return [1 << b for b in range(size.bit_length() - 1)]


def partner(value, x_mask, y_mask=0):
    x_size, y_size = lax.axis_size("gx"), lax.axis_size("gy")
    pairs = [
        (x * y_size + y, (x ^ x_mask) * y_size + (y ^ y_mask)) for x in range(x_size) for y in range(y_size)
    ]
    return lax.ppermute(value, ("gx", "gy"), pairs)


def summed(value):
    masks = [(bit, 0) for bit in bits(lax.axis_size("gx"))[1:]] + [(0, bit) for bit in bits(lax.axis_size("gy"))]
    while masks:
        first, masks = masks[0], masks[1:]
        near = value + partner(value, *first)
        if masks:
            second, masks = masks[0], masks[1:]
            both = (first[0] ^ second[0], first[1] ^ second[1])
            near = near + (partner(value, *second) + partner(value, *both))
        value = near
    return value


def in_two(value):
    high = value.astype(BF16)
    return high, (value - high.astype(F32)).astype(BF16)


def tiles(value):
    rows, columns = value.shape
    return [
        [value[r : r + SUBLANES, c : min(c + LANES, columns)] for c in range(0, columns, LANES)]
        for r in range(0, rows, SUBLANES)
    ]


def joined(groups):
    return jnp.concatenate([jnp.concatenate(group, axis=1) for group in groups], axis=0)


def eliminated(gram, extra):
    gram = [list(group) for group in gram]
    extra = [list(group) for group in extra]
    row_id = lax.broadcasted_iota(jnp.int32, (SUBLANES, LANES), 0)

    def row(tile, r):
        return jnp.broadcast_to(tile[r : r + 1, :], tile.shape)

    def column(tile, c):
        return jnp.broadcast_to(tile[:, c : c + 1], (SUBLANES, LANES))

    def spread(tile, r):
        return jnp.take_along_axis(tile, jnp.full(tile.shape, r, jnp.int32), axis=0)

    def less(tile, factor, other):
        return tile - factor[:, : tile.shape[1]] * other

    for g in range(len(gram)):
        at, first = divmod(g * SUBLANES, LANES)
        both = [gram[h] + extra[h] for h in range(len(gram))]
        rows = [[row(t, q) for t in both[g]] for q in range(SUBLANES)]
        pivots = [column(gram[g][at], first + b) for b in range(SUBLANES)]
        block = [[spread(pivots[b], a) if b >= a else None for b in range(SUBLANES)] for a in range(SUBLANES)]
        below = range(g + 1, len(gram))
        columns = {h: [column(gram[h][at], first + q) for q in range(SUBLANES)] for h in below}
        scales, inverses = [], []
        for q in range(SUBLANES):
            scales.append(lax.rsqrt(block[q][q]))
            inverses.append(scales[q] * scales[q])
            for b in range(q + 1, SUBLANES):
                factor = block[q][b] * inverses[q]
                for c in range(b, SUBLANES):
                    block[b][c] = block[b][c] - factor * block[q][c]
                rows[b] = [less(t, factor, r) for t, r in zip(rows[b], rows[q])]
                for h in below:
                    columns[h][b] = columns[h][b] - factor * columns[h][q]
        for h in below:
            for q in range(SUBLANES):
                factor = columns[h][q] * inverses[q]
                both[h] = [less(t, factor, r) for t, r in zip(both[h], rows[q])]
        for q in range(SUBLANES):
            both[g] = [
                jnp.where((row_id == q)[:, : t.shape[1]], r * scales[q][:, : t.shape[1]], t)
                for t, r in zip(both[g], rows[q])
            ]
        for h in range(g, len(gram)):
            gram[h], extra[h] = both[h][: len(gram[h])], both[h][len(gram[h]) :]
    return gram, extra


def orth_pass(rows, *more):
    inner_gram = lax.dot_general(rows, rows, ROWS_BY_ROWS, precision=precise, preferred_element_type=F32)
    widths = [v.shape[1] for v in (rows, *more)]
    extra = [sum(parts, []) for parts in zip(*(tiles(v) for v in (rows, *more)))]
    groups = eliminated(tiles(inner_gram), extra)[1]
    out, at = [], 0
    for width in widths:
        count = -(-width // LANES)
        out.append(joined([group[at : at + count] for group in groups]))
        at += count
    return out


def triangle_ids(n):
    return lax.broadcasted_iota(jnp.int32, (n, n), 0), lax.broadcasted_iota(jnp.int32, (n, n), 1)


def folded(full):
    half = full.shape[0] // 2
    r, c = triangle_ids(half)
    corner = full[half:, half:]
    diagonal = jnp.sum(jnp.where(r == c, corner, 0.0), axis=0, keepdims=True)
    return jnp.where(r > c, corner, full[:half, :half]), full[:half, half:], diagonal


def opened(fold, upper, diagonal):
    half = fold.shape[0]
    r, c = triangle_ids(half)
    turned = fold.T
    first = jnp.where(c >= r, fold, turned)
    second = jnp.where(r > c, fold, jnp.where(r == c, jnp.broadcast_to(diagonal, fold.shape), turned))
    return jnp.concatenate(
        [jnp.concatenate([first, upper], axis=1), jnp.concatenate([upper.T, second], axis=1)], axis=0
    )


def species_weights(rows, repeat):
    high, low = in_two(jnp.concatenate([rows] * repeat, axis=0).T)
    weights = jnp.concatenate([high, low], axis=1)
    return jnp.concatenate([weights, weights], axis=0)


def times(value, weights):
    out = jnp.dot(jnp.concatenate(in_two(value), axis=1), weights, preferred_element_type=F32)
    half = out.shape[1] // 2
    return out[:, :half] + out[:, half:]


def packed(narrow, first, count, stride, rank):
    lane = lax.broadcasted_iota(jnp.int32, (count, LANES), 1)
    pack = LANES // rank
    out = narrow[pl.ds(first + pack - 1, count, stride=stride), :]
    for q in range(pack - 2, -1, -1):
        out = jnp.where(lane < (q + 1) * rank, narrow[pl.ds(first + q, count, stride=stride), :], out)
    return out


def gram_kernel(cuts, place, field, mine, other, held, arrived):
    copies = [
        pltpu.make_async_copy(field.at[a:b], held.at[a:b], arrived.at[i])
        for i, (a, b) in enumerate(zip(cuts[:-1], cuts[1:]))
    ]
    for copy in copies:
        copy.start()
    square = cross = 0.0
    for copy, a, b in zip(copies, cuts[:-1], cuts[1:]):
        copy.wait()
        high, low = in_two(held[a:b])
        square = square + lax.dot_general(high, high, COLUMNS_BY_COLUMNS, preferred_element_type=F32)
        cross = cross + lax.dot_general(high, low, COLUMNS_BY_COLUMNS, preferred_element_type=F32)
    fold, upper, diagonal = folded(square + (cross + cross.T))
    half = fold.shape[0]
    edge = SUBLANES
    even = place[0] & 1 == 0

    def put(first, second):
        first[:half] = fold
        first[half:] = upper[:edge]
        second[: half - edge] = upper[edge:]
        second[half - edge :] = jnp.broadcast_to(diagonal, (2 * edge, half))

    @pl.when(even)
    def _():
        put(mine, other)

    @pl.when(jnp.logical_not(even))
    def _():
        put(other, mine)


def local_gram(place, unfolded):
    rows, z = unfolded.shape
    cuts = [0, rows // 8, rows // 2, rows]
    out = jax.ShapeDtypeStruct((z // 2 + SUBLANES, z // 2), F32)
    return pl.pallas_call(
        functools.partial(gram_kernel, cuts),
        out_shape=[out, out, jax.ShapeDtypeStruct((rows, z), F32)],
        in_specs=[SMEM, HBM],
        out_specs=[VMEM] * 3,
        scratch_shapes=[pltpu.SemaphoreType.DMA((len(cuts) - 1,))],
        compiler_params=pltpu.CompilerParams(vmem_limit_bytes=32 << 20),
        name="gram",
    )(place, unfolded)


def begin_kernel(place, mine, other, start, basis, image, gram):
    half = mine.shape[1]
    edge = SUBLANES
    even = place[0] & 1 == 0
    first = jnp.where(even, mine[...], other[...])
    second = jnp.where(even, other[...], mine[...])
    gram[...] = opened(
        first[:half],
        jnp.concatenate([first[half:], second[: half - edge]], axis=0),
        second[half - edge : half - edge + 1],
    )
    basis[...] = start[...]

    def multiplied():
        return jnp.dot(basis[...], gram[...], precision=precise, preferred_element_type=F32)

    @pl.loop(0, ITERS - 2)
    def _(iteration):
        basis[...] = orth_pass(*orth_pass(multiplied()))[0]

    basis[...] = orth_pass(multiplied())[0]
    image[...] = multiplied()


def begin(place, mine, other, start_rows):
    z = start_rows.shape[1]
    rows = jax.ShapeDtypeStruct(start_rows.shape, F32)
    return pl.pallas_call(
        begin_kernel,
        out_shape=[rows, rows, jax.ShapeDtypeStruct((z, z), F32)],
        in_specs=[SMEM] + [VMEM] * 3,
        out_specs=[VMEM] * 3,
        compiler_params=SMALL,
        name="begin",
    )(place, mine, other, start_rows)


def finish_kernel(basis, gram, out, again, factor):
    rank = basis.shape[0]
    r, c = triangle_ids(rank)
    rows, turn = orth_pass(basis[...], jnp.where(r == c, 1.0, 0.0))
    rows = jnp.dot(rows, gram[...], precision=precise, preferred_element_type=F32)
    for _ in range(2):
        rows, turn = orth_pass(rows, turn)
    out[...] = rows
    again[...] = rows
    factor[...] = turn


def finish(basis, gram):
    rank, z = basis.shape
    return pl.pallas_call(
        finish_kernel,
        out_shape=[jax.ShapeDtypeStruct((rank, z), F32)] * 2 + [jax.ShapeDtypeStruct((rank, rank), F32)],
        in_specs=[VMEM] * 2,
        out_specs=[VMEM] * 3,
        compiler_params=SMALL,
        cost_estimate=pl.CostEstimate(flops=1 << 30, bytes_accessed=1 << 24, transcendentals=0),
        name="finish",
    )(basis, gram)


def ahead_kernel(d, share, skip, species, place, field, image, out, narrow):
    count, x_cells, width = out.shape
    rank = image.shape[0]
    across = count * species
    start = pl.multiple_of(((place[0] ^ d) * share + skip) * species, species)
    cells = field[:, pl.ds(start, across), :]
    narrow[...] = times(cells.reshape(x_cells * across, cells.shape[2]), species_weights(image[...], LANES // rank))
    for y in range(count):
        for t in range(width // LANES):
            out[y, :, t * LANES : (t + 1) * LANES] = packed(
                narrow, y * species + t * (LANES // rank), x_cells, across, rank
            )


def contract_ahead(place, field, image, x_cells, y_cells, species, share, d, skip, count):
    z = field.shape[1]
    rank = image.shape[0]
    return pl.pallas_call(
        functools.partial(ahead_kernel, d, share, skip, species),
        out_shape=jax.ShapeDtypeStruct((count, x_cells, species * rank), F32),
        in_specs=[SMEM, VMEM, VMEM],
        out_specs=VMEM,
        scratch_shapes=[pltpu.VMEM((x_cells * count * species, LANES), F32)],
        compiler_params=SMALL,
        cost_estimate=pl.CostEstimate(flops=1 << 30, bytes_accessed=1 << 22, transcendentals=0),
    )(place, field.reshape(x_cells, y_cells * species, z), image)


def core_kernel(species, y_cells, place, field, basis, core, *refs):
    outs, (weights, narrow, strip) = refs[:-3], refs[-3:]
    share, step, width = outs[0].shape
    rank = basis.shape[0]
    cells = core.shape[0]
    half = len(outs)
    near = place[0] // half * half

    @pl.when(pl.program_id(0) == 0)
    def _():
        weights[...] = species_weights(basis[...], LANES // rank)

    block = narrow.shape[0]
    narrow[...] = times(field[pl.ds(pl.multiple_of(pl.program_id(0) * block, block), block), :], weights[...])
    for t in range(width // LANES):
        lanes = slice(t * LANES, (t + 1) * LANES)
        strip[...] = packed(narrow, t * (LANES // rank), cells, species, rank)
        core[:, lanes] = strip[...]
        for d, out in enumerate(outs):
            part = near + ((place[0] ^ d) & (half - 1))
            for y in range(share):
                out[y, :, lanes] = strip[pl.ds(part * share + y, step, stride=y_cells), :]


def contract(place, unfolded, basis, x_cells, y_cells, species, x_parts):
    rows, z = unfolded.shape
    rank = basis.shape[0]
    steps = 4
    block, cells = rows // steps, rows // species // steps
    width = species * rank
    share = y_cells // x_parts
    pieces = x_parts // 2
    return pl.pallas_call(
        functools.partial(core_kernel, species, y_cells),
        grid=(steps,),
        out_shape=[jax.ShapeDtypeStruct((rows // species, width), F32)]
        + [jax.ShapeDtypeStruct((share, x_cells, width), F32)] * pieces,
        in_specs=[
            SMEM,
            VMEM,
            pl.BlockSpec((rank, z), lambda i: (0, 0)),
        ],
        out_specs=[pl.BlockSpec((cells, width), lambda i: (i, 0))]
        + [pl.BlockSpec((share, x_cells // steps, width), lambda i: (0, i, 0))] * pieces,
        scratch_shapes=[
            pltpu.VMEM((2 * z, 2 * LANES), BF16),
            pltpu.VMEM((block, LANES), F32),
            pltpu.VMEM((cells, LANES), F32),
        ],
        compiler_params=SMALL,
        cost_estimate=pl.CostEstimate(flops=1 << 31, bytes_accessed=1 << 24, transcendentals=0),
        name="core",
    )(place, unfolded, basis)


def product_kernel(near_count, place, factor, *refs):
    near, far, (out, turn) = refs[:near_count], refs[near_count:-2], refs[-2:]
    share, size, width = near[0].shape
    rank = factor.shape[0]
    turn[...] = jnp.zeros_like(turn)
    for part, value in enumerate(in_two(factor[...])):
        for side in range(2):
            for q in range(LANES // rank):
                turn[
                    part * LANES + q * rank : part * LANES + (q + 1) * rank,
                    side * LANES + q * rank : side * LANES + (q + 1) * rank,
                ] = value
    strips = [
        piece[y, :, t : t + LANES]
        for piece in far
        for y in range(piece.shape[0])
        for t in range(0, width, LANES)
    ]
    both = jnp.concatenate(in_two(jnp.concatenate(strips, axis=0)), axis=1)
    turned = lax.dot_general(both, turn[...], ROWS_BY_ROWS, preferred_element_type=F32)
    turned = turned[:, :LANES] + turned[:, LANES:]
    count = width // LANES
    square = cross = 0.0
    for y in range(share):
        rows = [piece[y] for piece in near]
        for d in range(near_count):
            at = (d * share + y) * count
            rows.append(
                jnp.concatenate([turned[(at + t) * size : (at + t + 1) * size] for t in range(count)], axis=1)
            )
        high, low = in_two(jnp.concatenate(rows, axis=0))
        square = square + lax.dot_general(high, high, ROWS_BY_ROWS, preferred_element_type=F32)
        cross = cross + lax.dot_general(high, low, ROWS_BY_ROWS, preferred_element_type=F32)
    total = square + (cross + cross.T)
    for bit in bits(2 * near_count):
        step = size * bit
        swap = place[0] & bit != 0
        for axis in (0, 1):
            parts = [lax.slice_in_dim(total, c, c + step, axis=axis) for c in range(0, total.shape[axis], step)]
            swapped = jnp.concatenate([parts[c ^ 1] for c in range(len(parts))], axis=axis)
            total = jnp.where(swap, swapped, total)
    fold, upper, diagonal = folded(total)
    half = fold.shape[0]
    out[:half] = jnp.concatenate([fold, upper], axis=1)
    out[half:] = jnp.broadcast_to(jnp.concatenate([diagonal, diagonal], axis=1), (SUBLANES, 2 * half))


def product(place, factor, near, far):
    n = 2 * len(near) * near[0].shape[1]
    return pl.pallas_call(
        functools.partial(product_kernel, len(near)),
        out_shape=jax.ShapeDtypeStruct((n // 2 + SUBLANES, n), F32),
        in_specs=[SMEM] + [VMEM] * (1 + len(near) + len(far)),
        out_specs=VMEM,
        scratch_shapes=[pltpu.VMEM((2 * LANES, 2 * LANES), BF16)],
        compiler_params=SMALL,
        name="product",
    )(place, factor, *near, *far)


def triangle_kernel(scale, gram, out):
    half = gram.shape[1] // 2
    full = opened(gram[:half, :half], gram[:half, half:], gram[half : half + 1, :half])
    upper = joined(eliminated(tiles(full), [[] for _ in range(0, 2 * half, SUBLANES)])[0])
    r, c = triangle_ids(2 * half)
    out[...] = jnp.where(c >= r, upper * scale, 0.0)


def triangle(gram, scale):
    n = gram.shape[1]
    return pl.pallas_call(
        functools.partial(triangle_kernel, scale),
        out_shape=jax.ShapeDtypeStruct((n, n), F32),
        in_specs=[VMEM],
        out_specs=VMEM,
        compiler_params=SMALL,
        name="triangle",
    )(gram)


def local(state_field, start_basis):
    x_cells, y_cells, species, z_cells = state_field.shape
    rank_kept = start_basis.shape[1]
    unfolded = state_field.reshape(x_cells * y_cells * species, z_cells)
    x_parts = lax.axis_size("gx")
    place = lax.axis_index("gx").astype(jnp.int32).reshape(1)
    mine, other, held = local_gram(place, pltpu.with_memory_space_constraint(unfolded, pltpu.HBM))
    mine = summed(mine + partner(other, 1))
    other = partner(mine, 1)
    basis, image, gram = begin(place, mine, other, start_basis.T)
    far = []
    share = y_cells // x_parts
    for d, skip, count in far_pieces(x_parts, share):
        piece = contract_ahead(place, held, image, x_cells, y_cells, species, share, d, skip, count)
        far.append(partner(piece, d))
    basis_rows, basis, factor = finish(basis, gram)
    core_tensor, *near = contract(place, held, basis, x_cells, y_cells, species, x_parts)
    near = [partner(piece, d) if d else piece for d, piece in enumerate(near)]
    gram_x = product(place, factor, near, far)
    gram_x = summed(gram_x + partner(gram_x, 1))
    column_count = y_cells * lax.axis_size("gy") * species * rank_kept
    x_triangle = triangle(gram_x, 1.0 / column_count**0.5)
    return (core_tensor.reshape(x_cells, y_cells, species * rank_kept), basis_rows.T, x_triangle)


def far_pieces(x_parts, share):
    return [(d, 0, share) for d in range(x_parts // 2, x_parts)]


def solution(mesh):
    return jax.shard_map(
        local,
        mesh=mesh,
        in_specs=(P("gx", "gy", None, None), P()),
        out_specs=(P("gx", "gy", None), P(), P()),
        check_vma=False,
    )
```

```python
import functools

import jax
import jax.numpy as jnp
from jax import lax
from jax.experimental import pallas as pl
from jax.experimental.pallas import tpu as pltpu
from jax.sharding import PartitionSpec as P


ITERS = 3
F32, BF16 = jnp.float32, jnp.bfloat16
LANES, SUBLANES = 128, 8

precise = lax.Precision.HIGHEST
ROWS_BY_ROWS = (((1,), (1,)), ((), ()))
COLUMNS_BY_COLUMNS = (((0,), (0,)), ((), ()))
VMEM = pl.BlockSpec(memory_space=pltpu.VMEM)
SMEM = pl.BlockSpec(memory_space=pltpu.SMEM)
HBM = pl.BlockSpec(memory_space=pltpu.HBM)
SMALL = pltpu.CompilerParams(vmem_limit_bytes=32 << 20)


def bits(size):
    return [1 << b for b in range(size.bit_length() - 1)]


def partner(value, x_mask, y_mask=0):
    x_size, y_size = lax.axis_size("gx"), lax.axis_size("gy")
    pairs = [
        (x * y_size + y, (x ^ x_mask) * y_size + (y ^ y_mask)) for x in range(x_size) for y in range(y_size)
    ]
    return lax.ppermute(value, ("gx", "gy"), pairs)


def summed(value):
    masks = [(bit, 0) for bit in bits(lax.axis_size("gx"))[1:]] + [(0, bit) for bit in bits(lax.axis_size("gy"))]
    while masks:
        first, masks = masks[0], masks[1:]
        near = value + partner(value, *first)
        if masks:
            second, masks = masks[0], masks[1:]
            both = (first[0] ^ second[0], first[1] ^ second[1])
            near = near + (partner(value, *second) + partner(value, *both))
        value = near
    return value


def in_two(value):
    high = value.astype(BF16)
    return high, (value - high.astype(F32)).astype(BF16)


def tiles(value):
    rows, columns = value.shape
    return [
        [value[r : r + SUBLANES, c : min(c + LANES, columns)] for c in range(0, columns, LANES)]
        for r in range(0, rows, SUBLANES)
    ]


def joined(groups):
    return jnp.concatenate([jnp.concatenate(group, axis=1) for group in groups], axis=0)


def eliminated(gram, extra):
    gram = [list(group) for group in gram]
    extra = [list(group) for group in extra]
    row_id = lax.broadcasted_iota(jnp.int32, (SUBLANES, LANES), 0)

    def row(tile, r):
        return jnp.broadcast_to(tile[r : r + 1, :], tile.shape)

    def column(tile, c):
        return jnp.broadcast_to(tile[:, c : c + 1], (SUBLANES, LANES))

    def spread(tile, r):
        return jnp.take_along_axis(tile, jnp.full(tile.shape, r, jnp.int32), axis=0)

    def less(tile, factor, other):
        return tile - factor[:, : tile.shape[1]] * other

    for g in range(len(gram)):
        at, first = divmod(g * SUBLANES, LANES)
        both = [gram[h] + extra[h] for h in range(len(gram))]
        rows = [[row(t, q) for t in both[g]] for q in range(SUBLANES)]
        pivots = [column(gram[g][at], first + b) for b in range(SUBLANES)]
        block = [[spread(pivots[b], a) if b >= a else None for b in range(SUBLANES)] for a in range(SUBLANES)]
        below = range(g + 1, len(gram))
        columns = {h: [column(gram[h][at], first + q) for q in range(SUBLANES)] for h in below}
        scales, inverses = [], []
        for q in range(SUBLANES):
            scales.append(lax.rsqrt(block[q][q]))
            inverses.append(scales[q] * scales[q])
            for b in range(q + 1, SUBLANES):
                factor = block[q][b] * inverses[q]
                for c in range(b, SUBLANES):
                    block[b][c] = block[b][c] - factor * block[q][c]
                rows[b] = [less(t, factor, r) for t, r in zip(rows[b], rows[q])]
                for h in below:
                    columns[h][b] = columns[h][b] - factor * columns[h][q]
        for h in below:
            for q in range(SUBLANES):
                factor = columns[h][q] * inverses[q]
                both[h] = [less(t, factor, r) for t, r in zip(both[h], rows[q])]
        for q in range(SUBLANES):
            both[g] = [
                jnp.where((row_id == q)[:, : t.shape[1]], r * scales[q][:, : t.shape[1]], t)
                for t, r in zip(both[g], rows[q])
            ]
        for h in range(g, len(gram)):
            gram[h], extra[h] = both[h][: len(gram[h])], both[h][len(gram[h]) :]
    return gram, extra


def orth_pass(rows, *more):
    inner_gram = lax.dot_general(rows, rows, ROWS_BY_ROWS, precision=precise, preferred_element_type=F32)
    widths = [v.shape[1] for v in (rows, *more)]
    extra = [sum(parts, []) for parts in zip(*(tiles(v) for v in (rows, *more)))]
    groups = eliminated(tiles(inner_gram), extra)[1]
    out, at = [], 0
    for width in widths:
        count = -(-width // LANES)
        out.append(joined([group[at : at + count] for group in groups]))
        at += count
    return out


def triangle_ids(n):
    return lax.broadcasted_iota(jnp.int32, (n, n), 0), lax.broadcasted_iota(jnp.int32, (n, n), 1)


def folded(full):
    half = full.shape[0] // 2
    r, c = triangle_ids(half)
    corner = full[half:, half:]
    diagonal = jnp.sum(jnp.where(r == c, corner, 0.0), axis=0, keepdims=True)
    return jnp.where(r > c, corner, full[:half, :half]), full[:half, half:], diagonal


def opened(fold, upper, diagonal):
    half = fold.shape[0]
    r, c = triangle_ids(half)
    turned = fold.T
    first = jnp.where(c >= r, fold, turned)
    second = jnp.where(r > c, fold, jnp.where(r == c, jnp.broadcast_to(diagonal, fold.shape), turned))
    return jnp.concatenate(
        [jnp.concatenate([first, upper], axis=1), jnp.concatenate([upper.T, second], axis=1)], axis=0
    )


def species_weights(rows, repeat):
    high, low = in_two(jnp.concatenate([rows] * repeat, axis=0).T)
    weights = jnp.concatenate([high, low], axis=1)
    return jnp.concatenate([weights, weights], axis=0)


def times(value, weights):
    out = jnp.dot(jnp.concatenate(in_two(value), axis=1), weights, preferred_element_type=F32)
    half = out.shape[1] // 2
    return out[:, :half] + out[:, half:]


def packed(narrow, first, count, stride, rank):
    lane = lax.broadcasted_iota(jnp.int32, (count, LANES), 1)
    pack = LANES // rank
    out = narrow[pl.ds(first + pack - 1, count, stride=stride), :]
    for q in range(pack - 2, -1, -1):
        out = jnp.where(lane < (q + 1) * rank, narrow[pl.ds(first + q, count, stride=stride), :], out)
    return out


def gram_kernel(cuts, place, field, mine, other, held, arrived):
    copies = [
        pltpu.make_async_copy(field.at[a:b], held.at[a:b], arrived.at[i])
        for i, (a, b) in enumerate(zip(cuts[:-1], cuts[1:]))
    ]
    for copy in copies:
        copy.start()
    total = 0.0
    for copy, a, b in zip(copies, cuts[:-1], cuts[1:]):
        copy.wait()
        high, low = in_two(held[a:b])
        total = total + lax.dot_general(
            high, jnp.concatenate([high, low], axis=1), COLUMNS_BY_COLUMNS, preferred_element_type=F32
        )
    square, cross = jnp.split(total, 2, axis=1)
    fold, upper, diagonal = folded(square + (cross + cross.T))
    half = fold.shape[0]
    edge = SUBLANES
    even = place[0] & 1 == 0

    def put(first, second):
        first[:half] = fold
        first[half:] = upper[:edge]
        second[: half - edge] = upper[edge:]
        second[half - edge :] = jnp.broadcast_to(diagonal, (2 * edge, half))

    @pl.when(even)
    def _():
        put(mine, other)

    @pl.when(jnp.logical_not(even))
    def _():
        put(other, mine)


def local_gram(place, unfolded):
    rows, z = unfolded.shape
    cuts = [0, rows // 8, rows // 2, rows]
    out = jax.ShapeDtypeStruct((z // 2 + SUBLANES, z // 2), F32)
    return pl.pallas_call(
        functools.partial(gram_kernel, cuts),
        out_shape=[out, out, jax.ShapeDtypeStruct((rows, z), F32)],
        in_specs=[SMEM, HBM],
        out_specs=[VMEM] * 3,
        scratch_shapes=[pltpu.SemaphoreType.DMA((len(cuts) - 1,))],
        compiler_params=pltpu.CompilerParams(vmem_limit_bytes=32 << 20),
        name="gram",
    )(place, unfolded)


def begin_kernel(place, mine, other, start, basis, image, gram):
    half = mine.shape[1]
    edge = SUBLANES
    even = place[0] & 1 == 0
    first = jnp.where(even, mine[...], other[...])
    second = jnp.where(even, other[...], mine[...])
    gram[...] = opened(
        first[:half],
        jnp.concatenate([first[half:], second[: half - edge]], axis=0),
        second[half - edge : half - edge + 1],
    )
    basis[...] = start[...]

    def multiplied():
        return jnp.dot(basis[...], gram[...], precision=precise, preferred_element_type=F32)

    @pl.loop(0, ITERS - 2)
    def _(iteration):
        basis[...] = orth_pass(*orth_pass(multiplied()))[0]

    basis[...] = orth_pass(multiplied())[0]
    image[...] = multiplied()


def begin(place, mine, other, start_rows):
    z = start_rows.shape[1]
    rows = jax.ShapeDtypeStruct(start_rows.shape, F32)
    return pl.pallas_call(
        begin_kernel,
        out_shape=[rows, rows, jax.ShapeDtypeStruct((z, z), F32)],
        in_specs=[SMEM] + [VMEM] * 3,
        out_specs=[VMEM] * 3,
        compiler_params=SMALL,
        name="begin",
    )(place, mine, other, start_rows)


def finish_kernel(basis, gram, out, again, factor):
    rank = basis.shape[0]
    r, c = triangle_ids(rank)
    rows, turn = orth_pass(basis[...], jnp.where(r == c, 1.0, 0.0))
    rows = jnp.dot(rows, gram[...], precision=precise, preferred_element_type=F32)
    for _ in range(2):
        rows, turn = orth_pass(rows, turn)
    out[...] = rows
    again[...] = rows
    factor[...] = turn


def finish(basis, gram):
    rank, z = basis.shape
    return pl.pallas_call(
        finish_kernel,
        out_shape=[jax.ShapeDtypeStruct((rank, z), F32)] * 2 + [jax.ShapeDtypeStruct((rank, rank), F32)],
        in_specs=[VMEM] * 2,
        out_specs=[VMEM] * 3,
        compiler_params=SMALL,
        cost_estimate=pl.CostEstimate(flops=1 << 30, bytes_accessed=1 << 24, transcendentals=0),
        name="finish",
    )(basis, gram)


def ahead_kernel(d, share, skip, species, place, field, image, out, narrow):
    count, x_cells, width = out.shape
    rank = image.shape[0]
    across = count * species
    start = pl.multiple_of(((place[0] ^ d) * share + skip) * species, species)
    cells = field[:, pl.ds(start, across), :]
    narrow[...] = times(cells.reshape(x_cells * across, cells.shape[2]), species_weights(image[...], LANES // rank))
    for y in range(count):
        for t in range(width // LANES):
            out[y, :, t * LANES : (t + 1) * LANES] = packed(
                narrow, y * species + t * (LANES // rank), x_cells, across, rank
            )


def contract_ahead(place, field, image, x_cells, y_cells, species, share, d, skip, count):
    z = field.shape[1]
    rank = image.shape[0]
    return pl.pallas_call(
        functools.partial(ahead_kernel, d, share, skip, species),
        out_shape=jax.ShapeDtypeStruct((count, x_cells, species * rank), F32),
        in_specs=[SMEM, VMEM, VMEM],
        out_specs=VMEM,
        scratch_shapes=[pltpu.VMEM((x_cells * count * species, LANES), F32)],
        compiler_params=SMALL,
        cost_estimate=pl.CostEstimate(flops=1 << 30, bytes_accessed=1 << 22, transcendentals=0),
    )(place, field.reshape(x_cells, y_cells * species, z), image)


def core_kernel(species, y_cells, place, field, basis, core, *refs):
    outs, (weights, narrow, strip) = refs[:-3], refs[-3:]
    share, step, width = outs[0].shape
    rank = basis.shape[0]
    cells = core.shape[0]
    half = len(outs)
    near = place[0] // half * half

    @pl.when(pl.program_id(0) == 0)
    def _():
        weights[...] = species_weights(basis[...], LANES // rank)

    block = narrow.shape[0]
    narrow[...] = times(field[pl.ds(pl.multiple_of(pl.program_id(0) * block, block), block), :], weights[...])
    for t in range(width // LANES):
        lanes = slice(t * LANES, (t + 1) * LANES)
        strip[...] = packed(narrow, t * (LANES // rank), cells, species, rank)
        core[:, lanes] = strip[...]
        for d, out in enumerate(outs):
            part = near + ((place[0] ^ d) & (half - 1))
            for y in range(share):
                out[y, :, lanes] = strip[pl.ds(part * share + y, step, stride=y_cells), :]


def contract(place, unfolded, basis, x_cells, y_cells, species, x_parts):
    rows, z = unfolded.shape
    rank = basis.shape[0]
    steps = 4
    block, cells = rows // steps, rows // species // steps
    width = species * rank
    share = y_cells // x_parts
    pieces = x_parts // 2
    return pl.pallas_call(
        functools.partial(core_kernel, species, y_cells),
        grid=(steps,),
        out_shape=[jax.ShapeDtypeStruct((rows // species, width), F32)]
        + [jax.ShapeDtypeStruct((share, x_cells, width), F32)] * pieces,
        in_specs=[
            SMEM,
            VMEM,
            pl.BlockSpec((rank, z), lambda i: (0, 0)),
        ],
        out_specs=[pl.BlockSpec((cells, width), lambda i: (i, 0))]
        + [pl.BlockSpec((share, x_cells // steps, width), lambda i: (0, i, 0))] * pieces,
        scratch_shapes=[
            pltpu.VMEM((2 * z, 2 * LANES), BF16),
            pltpu.VMEM((block, LANES), F32),
            pltpu.VMEM((cells, LANES), F32),
        ],
        compiler_params=SMALL,
        cost_estimate=pl.CostEstimate(flops=1 << 31, bytes_accessed=1 << 24, transcendentals=0),
        name="core",
    )(place, unfolded, basis)


def product_kernel(near_count, place, factor, *refs):
    near, far, (out, turn) = refs[:near_count], refs[near_count:-2], refs[-2:]
    share, size, width = near[0].shape
    rank = factor.shape[0]
    turn[...] = jnp.zeros_like(turn)
    for part, value in enumerate(in_two(factor[...])):
        for side in range(2):
            for q in range(LANES // rank):
                turn[
                    part * LANES + q * rank : part * LANES + (q + 1) * rank,
                    side * LANES + q * rank : side * LANES + (q + 1) * rank,
                ] = value
    strips = [
        piece[y, :, t : t + LANES]
        for piece in far
        for y in range(piece.shape[0])
        for t in range(0, width, LANES)
    ]
    both = jnp.concatenate(in_two(jnp.concatenate(strips, axis=0)), axis=1)
    turned = lax.dot_general(both, turn[...], ROWS_BY_ROWS, preferred_element_type=F32)
    turned = turned[:, :LANES] + turned[:, LANES:]
    count = width // LANES
    columns = []
    for y in range(share):
        rows = [piece[y] for piece in near]
        for d in range(near_count):
            at = (d * share + y) * count
            rows.append(
                jnp.concatenate([turned[(at + t) * size : (at + t + 1) * size] for t in range(count)], axis=1)
            )
        columns.append(jnp.concatenate(rows, axis=0))
    high, low = in_two(jnp.concatenate(columns, axis=1))
    total = lax.dot_general(
        high, jnp.concatenate([high, low], axis=0), ROWS_BY_ROWS, preferred_element_type=F32
    )
    square, cross = jnp.split(total, 2, axis=1)
    total = square + (cross + cross.T)
    for bit in bits(2 * near_count):
        step = size * bit
        swap = place[0] & bit != 0
        for axis in (0, 1):
            parts = [lax.slice_in_dim(total, c, c + step, axis=axis) for c in range(0, total.shape[axis], step)]
            swapped = jnp.concatenate([parts[c ^ 1] for c in range(len(parts))], axis=axis)
            total = jnp.where(swap, swapped, total)
    fold, upper, diagonal = folded(total)
    half = fold.shape[0]
    out[:half] = jnp.concatenate([fold, upper], axis=1)
    out[half:] = jnp.broadcast_to(jnp.concatenate([diagonal, diagonal], axis=1), (SUBLANES, 2 * half))


def product(place, factor, near, far):
    n = 2 * len(near) * near[0].shape[1]
    return pl.pallas_call(
        functools.partial(product_kernel, len(near)),
        out_shape=jax.ShapeDtypeStruct((n // 2 + SUBLANES, n), F32),
        in_specs=[SMEM] + [VMEM] * (1 + len(near) + len(far)),
        out_specs=VMEM,
        scratch_shapes=[pltpu.VMEM((2 * LANES, 2 * LANES), BF16)],
        compiler_params=SMALL,
        name="product",
    )(place, factor, *near, *far)


def triangle_kernel(scale, gram, out):
    half = gram.shape[1] // 2
    full = opened(gram[:half, :half], gram[:half, half:], gram[half : half + 1, :half])
    upper = joined(eliminated(tiles(full), [[] for _ in range(0, 2 * half, SUBLANES)])[0])
    r, c = triangle_ids(2 * half)
    out[...] = jnp.where(c >= r, upper * scale, 0.0)


def triangle(gram, scale):
    n = gram.shape[1]
    return pl.pallas_call(
        functools.partial(triangle_kernel, scale),
        out_shape=jax.ShapeDtypeStruct((n, n), F32),
        in_specs=[VMEM],
        out_specs=VMEM,
        compiler_params=SMALL,
        name="triangle",
    )(gram)


def local(state_field, start_basis):
    x_cells, y_cells, species, z_cells = state_field.shape
    rank_kept = start_basis.shape[1]
    unfolded = state_field.reshape(x_cells * y_cells * species, z_cells)
    x_parts = lax.axis_size("gx")
    place = lax.axis_index("gx").astype(jnp.int32).reshape(1)
    mine, other, held = local_gram(place, pltpu.with_memory_space_constraint(unfolded, pltpu.HBM))
    mine = summed(mine + partner(other, 1))
    other = partner(mine, 1)
    basis, image, gram = begin(place, mine, other, start_basis.T)
    far = []
    share = y_cells // x_parts
    for d, skip, count in far_pieces(x_parts, share):
        piece = contract_ahead(place, held, image, x_cells, y_cells, species, share, d, skip, count)
        far.append(partner(piece, d))
    basis_rows, basis, factor = finish(basis, gram)
    core_tensor, *near = contract(place, held, basis, x_cells, y_cells, species, x_parts)
    near = [partner(piece, d) if d else piece for d, piece in enumerate(near)]
    gram_x = product(place, factor, near, far)
    gram_x = summed(gram_x + partner(gram_x, 1))
    column_count = y_cells * lax.axis_size("gy") * species * rank_kept
    x_triangle = triangle(gram_x, 1.0 / column_count**0.5)
    return (core_tensor.reshape(x_cells, y_cells, species * rank_kept), basis_rows.T, x_triangle)


def far_pieces(x_parts, share):
    return [(d, 0, share) for d in range(x_parts // 2, x_parts)]


def solution(mesh):
    return jax.shard_map(
        local,
        mesh=mesh,
        in_specs=(P("gx", "gy", None, None), P()),
        out_specs=(P("gx", "gy", None), P(), P()),
        check_vma=False,
    )
```

```python
import functools

import jax
import jax.numpy as jnp
from jax import lax
from jax.experimental import pallas as pl
from jax.experimental.pallas import tpu as pltpu
from jax.sharding import PartitionSpec as P


ITERS = 3
F32, BF16 = jnp.float32, jnp.bfloat16
LANES, SUBLANES = 128, 8

precise = lax.Precision.HIGHEST
ROWS_BY_ROWS = (((1,), (1,)), ((), ()))
COLUMNS_BY_COLUMNS = (((0,), (0,)), ((), ()))
VMEM = pl.BlockSpec(memory_space=pltpu.VMEM)
SMEM = pl.BlockSpec(memory_space=pltpu.SMEM)
HBM = pl.BlockSpec(memory_space=pltpu.HBM)
SMALL = pltpu.CompilerParams(vmem_limit_bytes=32 << 20)


def bits(size):
    return [1 << b for b in range(size.bit_length() - 1)]


def partner(value, x_mask, y_mask=0):
    x_size, y_size = lax.axis_size("gx"), lax.axis_size("gy")
    pairs = [
        (x * y_size + y, (x ^ x_mask) * y_size + (y ^ y_mask)) for x in range(x_size) for y in range(y_size)
    ]
    return lax.ppermute(value, ("gx", "gy"), pairs)


def summed(value):
    masks = [(bit, 0) for bit in bits(lax.axis_size("gx"))[1:]] + [(0, bit) for bit in bits(lax.axis_size("gy"))]
    while masks:
        first, masks = masks[0], masks[1:]
        near = value + partner(value, *first)
        if masks:
            second, masks = masks[0], masks[1:]
            both = (first[0] ^ second[0], first[1] ^ second[1])
            near = near + (partner(value, *second) + partner(value, *both))
        value = near
    return value


def in_two(value):
    high = value.astype(BF16)
    return high, (value - high.astype(F32)).astype(BF16)


def tiles(value):
    rows, columns = value.shape
    return [
        [value[r : r + SUBLANES, c : min(c + LANES, columns)] for c in range(0, columns, LANES)]
        for r in range(0, rows, SUBLANES)
    ]


def joined(groups):
    return jnp.concatenate([jnp.concatenate(group, axis=1) for group in groups], axis=0)


def eliminated(gram, extra):
    gram = [list(group) for group in gram]
    extra = [list(group) for group in extra]
    row_id = lax.broadcasted_iota(jnp.int32, (SUBLANES, LANES), 0)

    def row(tile, r):
        return jnp.broadcast_to(tile[r : r + 1, :], tile.shape)

    def column(tile, c):
        return jnp.broadcast_to(tile[:, c : c + 1], (SUBLANES, LANES))

    def spread(tile, r):
        return jnp.take_along_axis(tile, jnp.full(tile.shape, r, jnp.int32), axis=0)

    def less(tile, factor, other):
        return tile - factor[:, : tile.shape[1]] * other

    for g in range(len(gram)):
        at, first = divmod(g * SUBLANES, LANES)
        both = [gram[h] + extra[h] for h in range(len(gram))]
        rows = [[row(t, q) for t in both[g]] for q in range(SUBLANES)]
        pivots = [column(gram[g][at], first + b) for b in range(SUBLANES)]
        block = [[spread(pivots[b], a) if b >= a else None for b in range(SUBLANES)] for a in range(SUBLANES)]
        below = range(g + 1, len(gram))
        columns = {h: [column(gram[h][at], first + q) for q in range(SUBLANES)] for h in below}
        scales, inverses = [], []
        for q in range(SUBLANES):
            scales.append(lax.rsqrt(block[q][q]))
            inverses.append(scales[q] * scales[q])
            for b in range(q + 1, SUBLANES):
                factor = block[q][b] * inverses[q]
                for c in range(b, SUBLANES):
                    block[b][c] = block[b][c] - factor * block[q][c]
                rows[b] = [less(t, factor, r) for t, r in zip(rows[b], rows[q])]
                for h in below:
                    columns[h][b] = columns[h][b] - factor * columns[h][q]
        for h in below:
            for q in range(SUBLANES):
                factor = columns[h][q] * inverses[q]
                both[h] = [less(t, factor, r) for t, r in zip(both[h], rows[q])]
        for q in range(SUBLANES):
            both[g] = [
                jnp.where((row_id == q)[:, : t.shape[1]], r * scales[q][:, : t.shape[1]], t)
                for t, r in zip(both[g], rows[q])
            ]
        for h in range(g, len(gram)):
            gram[h], extra[h] = both[h][: len(gram[h])], both[h][len(gram[h]) :]
    return gram, extra


def orth_pass(rows, *more):
    inner_gram = lax.dot_general(rows, rows, ROWS_BY_ROWS, precision=precise, preferred_element_type=F32)
    widths = [v.shape[1] for v in (rows, *more)]
    extra = [sum(parts, []) for parts in zip(*(tiles(v) for v in (rows, *more)))]
    groups = eliminated(tiles(inner_gram), extra)[1]
    out, at = [], 0
    for width in widths:
        count = -(-width // LANES)
        out.append(joined([group[at : at + count] for group in groups]))
        at += count
    return out


def triangle_ids(n):
    return lax.broadcasted_iota(jnp.int32, (n, n), 0), lax.broadcasted_iota(jnp.int32, (n, n), 1)


def folded(full):
    half = full.shape[0] // 2
    r, c = triangle_ids(half)
    corner = full[half:, half:]
    diagonal = jnp.sum(jnp.where(r == c, corner, 0.0), axis=0, keepdims=True)
    return jnp.where(r > c, corner, full[:half, :half]), full[:half, half:], diagonal


def opened(fold, upper, diagonal):
    half = fold.shape[0]
    r, c = triangle_ids(half)
    turned = fold.T
    first = jnp.where(c >= r, fold, turned)
    second = jnp.where(r > c, fold, jnp.where(r == c, jnp.broadcast_to(diagonal, fold.shape), turned))
    return jnp.concatenate(
        [jnp.concatenate([first, upper], axis=1), jnp.concatenate([upper.T, second], axis=1)], axis=0
    )


def species_weights(rows, repeat):
    high, low = in_two(jnp.concatenate([rows] * repeat, axis=0).T)
    weights = jnp.concatenate([high, low], axis=1)
    return jnp.concatenate([weights, weights], axis=0)


def times(value, weights):
    out = jnp.dot(jnp.concatenate(in_two(value), axis=1), weights, preferred_element_type=F32)
    half = out.shape[1] // 2
    return out[:, :half] + out[:, half:]


def packed(narrow, first, count, stride, rank):
    lane = lax.broadcasted_iota(jnp.int32, (count, LANES), 1)
    pack = LANES // rank
    out = narrow[pl.ds(first + pack - 1, count, stride=stride), :]
    for q in range(pack - 2, -1, -1):
        out = jnp.where(lane < (q + 1) * rank, narrow[pl.ds(first + q, count, stride=stride), :], out)
    return out


def gram_kernel(cuts, place, field, mine, other, held, arrived):
    copies = [
        pltpu.make_async_copy(field.at[a:b], held.at[a:b], arrived.at[i])
        for i, (a, b) in enumerate(zip(cuts[:-1], cuts[1:]))
    ]
    for copy in copies:
        copy.start()
    total = 0.0
    for copy, a, b in zip(copies, cuts[:-1], cuts[1:]):
        copy.wait()
        high, low = in_two(held[a:b])
        total = total + lax.dot_general(
            high, jnp.concatenate([high, low], axis=1), COLUMNS_BY_COLUMNS, preferred_element_type=F32
        )
    square, cross = jnp.split(total, 2, axis=1)
    fold, upper, diagonal = folded(square + (cross + cross.T))
    half = fold.shape[0]
    edge = SUBLANES
    even = place[0] & 1 == 0

    def put(first, second):
        first[:half] = fold
        first[half:] = upper[:edge]
        second[: half - edge] = upper[edge:]
        second[half - edge :] = jnp.broadcast_to(diagonal, (2 * edge, half))

    @pl.when(even)
    def _():
        put(mine, other)

    @pl.when(jnp.logical_not(even))
    def _():
        put(other, mine)


def local_gram(place, unfolded):
    rows, z = unfolded.shape
    cuts = [0, rows // 8, rows // 2, rows]
    out = jax.ShapeDtypeStruct((z // 2 + SUBLANES, z // 2), F32)
    return pl.pallas_call(
        functools.partial(gram_kernel, cuts),
        out_shape=[out, out, jax.ShapeDtypeStruct((rows, z), F32)],
        in_specs=[SMEM, HBM],
        out_specs=[VMEM] * 3,
        scratch_shapes=[pltpu.SemaphoreType.DMA((len(cuts) - 1,))],
        compiler_params=pltpu.CompilerParams(vmem_limit_bytes=32 << 20),
        name="gram",
    )(place, unfolded)


def begin_kernel(place, mine, other, start, basis, image, gram):
    half = mine.shape[1]
    edge = SUBLANES
    even = place[0] & 1 == 0
    first = jnp.where(even, mine[...], other[...])
    second = jnp.where(even, other[...], mine[...])
    gram[...] = opened(
        first[:half],
        jnp.concatenate([first[half:], second[: half - edge]], axis=0),
        second[half - edge : half - edge + 1],
    )
    basis[...] = start[...]

    def multiplied():
        return jnp.dot(basis[...], gram[...], precision=precise, preferred_element_type=F32)

    @pl.loop(0, ITERS - 2)
    def _(iteration):
        basis[...] = orth_pass(*orth_pass(multiplied()))[0]

    basis[...] = orth_pass(multiplied())[0]
    image[...] = multiplied()


def begin(place, mine, other, start_rows):
    z = start_rows.shape[1]
    rows = jax.ShapeDtypeStruct(start_rows.shape, F32)
    return pl.pallas_call(
        begin_kernel,
        out_shape=[rows, rows, jax.ShapeDtypeStruct((z, z), F32)],
        in_specs=[SMEM] + [VMEM] * 3,
        out_specs=[VMEM] * 3,
        compiler_params=SMALL,
        name="begin",
    )(place, mine, other, start_rows)


def finish_kernel(basis, gram, out, again, factor):
    rank = basis.shape[0]
    r, c = triangle_ids(rank)
    rows, turn = orth_pass(basis[...], jnp.where(r == c, 1.0, 0.0))
    rows = jnp.dot(rows, gram[...], precision=precise, preferred_element_type=F32)
    for _ in range(2):
        rows, turn = orth_pass(rows, turn)
    out[...] = rows
    again[...] = rows
    factor[...] = turn


def finish(basis, gram):
    rank, z = basis.shape
    return pl.pallas_call(
        finish_kernel,
        out_shape=[jax.ShapeDtypeStruct((rank, z), F32)] * 2 + [jax.ShapeDtypeStruct((rank, rank), F32)],
        in_specs=[VMEM] * 2,
        out_specs=[VMEM] * 3,
        compiler_params=SMALL,
        cost_estimate=pl.CostEstimate(flops=1 << 30, bytes_accessed=1 << 24, transcendentals=0),
        name="finish",
    )(basis, gram)


def ahead_kernel(d, share, skip, species, place, field, image, out, narrow):
    count, x_cells, width = out.shape
    rank = image.shape[0]
    across = count * species
    start = pl.multiple_of(((place[0] ^ d) * share + skip) * species, species)
    cells = field[:, pl.ds(start, across), :]
    narrow[...] = times(cells.reshape(x_cells * across, cells.shape[2]), species_weights(image[...], LANES // rank))
    for y in range(count):
        for t in range(width // LANES):
            out[y, :, t * LANES : (t + 1) * LANES] = packed(
                narrow, y * species + t * (LANES // rank), x_cells, across, rank
            )


def contract_ahead(place, field, image, x_cells, y_cells, species, share, d, skip, count):
    z = field.shape[1]
    rank = image.shape[0]
    return pl.pallas_call(
        functools.partial(ahead_kernel, d, share, skip, species),
        out_shape=jax.ShapeDtypeStruct((count, x_cells, species * rank), F32),
        in_specs=[SMEM, VMEM, VMEM],
        out_specs=VMEM,
        scratch_shapes=[pltpu.VMEM((x_cells * count * species, LANES), F32)],
        compiler_params=SMALL,
        cost_estimate=pl.CostEstimate(flops=1 << 30, bytes_accessed=1 << 22, transcendentals=0),
    )(place, field.reshape(x_cells, y_cells * species, z), image)


def core_kernel(species, y_cells, place, field, basis, core, *refs):
    outs, (weights, narrow, strip) = refs[:-3], refs[-3:]
    share, step, width = outs[0].shape
    rank = basis.shape[0]
    cells = core.shape[0]
    half = len(outs)
    near = place[0] // half * half

    @pl.when(pl.program_id(0) == 0)
    def _():
        weights[...] = species_weights(basis[...], LANES // rank)

    block = narrow.shape[0]
    narrow[...] = times(field[pl.ds(pl.multiple_of(pl.program_id(0) * block, block), block), :], weights[...])
    for t in range(width // LANES):
        lanes = slice(t * LANES, (t + 1) * LANES)
        strip[...] = packed(narrow, t * (LANES // rank), cells, species, rank)
        core[:, lanes] = strip[...]
        for d, out in enumerate(outs):
            part = near + ((place[0] ^ d) & (half - 1))
            for y in range(share):
                out[y, :, lanes] = strip[pl.ds(part * share + y, step, stride=y_cells), :]


def contract(place, unfolded, basis, x_cells, y_cells, species, x_parts):
    rows, z = unfolded.shape
    rank = basis.shape[0]
    steps = 4
    block, cells = rows // steps, rows // species // steps
    width = species * rank
    share = y_cells // x_parts
    pieces = x_parts // 2
    return pl.pallas_call(
        functools.partial(core_kernel, species, y_cells),
        grid=(steps,),
        out_shape=[jax.ShapeDtypeStruct((rows // species, width), F32)]
        + [jax.ShapeDtypeStruct((share, x_cells, width), F32)] * pieces,
        in_specs=[
            SMEM,
            VMEM,
            pl.BlockSpec((rank, z), lambda i: (0, 0)),
        ],
        out_specs=[pl.BlockSpec((cells, width), lambda i: (i, 0))]
        + [pl.BlockSpec((share, x_cells // steps, width), lambda i: (0, i, 0))] * pieces,
        scratch_shapes=[
            pltpu.VMEM((2 * z, 2 * LANES), BF16),
            pltpu.VMEM((block, LANES), F32),
            pltpu.VMEM((cells, LANES), F32),
        ],
        compiler_params=SMALL,
        cost_estimate=pl.CostEstimate(flops=1 << 31, bytes_accessed=1 << 24, transcendentals=0),
        name="core",
    )(place, unfolded, basis)


def product_kernel(near_count, place, factor, *refs):
    near, far, (out, turn) = refs[:near_count], refs[near_count:-2], refs[-2:]
    share, size, width = near[0].shape
    rank = factor.shape[0]
    turn[...] = jnp.zeros_like(turn)
    for part, value in enumerate(in_two(factor[...])):
        for side in range(2):
            for q in range(LANES // rank):
                turn[
                    part * LANES + q * rank : part * LANES + (q + 1) * rank,
                    side * LANES + q * rank : side * LANES + (q + 1) * rank,
                ] = value
    strips = [
        piece[y, :, t : t + LANES]
        for piece in far
        for y in range(piece.shape[0])
        for t in range(0, width, LANES)
    ]
    both = jnp.concatenate(in_two(jnp.concatenate(strips, axis=0)), axis=1)
    turned = lax.dot_general(both, turn[...], ROWS_BY_ROWS, preferred_element_type=F32)
    turned = turned[:, :LANES] + turned[:, LANES:]
    count = width // LANES
    columns = []
    for y in range(share):
        rows = [piece[y] for piece in near]
        for d in range(near_count):
            at = (d * share + y) * count
            rows.append(
                jnp.concatenate([turned[(at + t) * size : (at + t + 1) * size] for t in range(count)], axis=1)
            )
        columns.append(jnp.concatenate(rows, axis=0))
    high, low = in_two(jnp.concatenate(columns, axis=1))
    total = lax.dot_general(
        high, jnp.concatenate([high, low], axis=0), ROWS_BY_ROWS, preferred_element_type=F32
    )
    square, cross = jnp.split(total, 2, axis=1)
    total = square + (cross + cross.T)
    for bit in bits(2 * near_count):
        step = size * bit
        swap = place[0] & bit != 0
        for axis in (0, 1):
            parts = [lax.slice_in_dim(total, c, c + step, axis=axis) for c in range(0, total.shape[axis], step)]
            swapped = jnp.concatenate([parts[c ^ 1] for c in range(len(parts))], axis=axis)
            total = jnp.where(swap, swapped, total)
    fold, upper, diagonal = folded(total)
    half = fold.shape[0]
    out[:half] = jnp.concatenate([fold, upper], axis=1)
    out[half:] = jnp.broadcast_to(jnp.concatenate([diagonal, diagonal], axis=1), (SUBLANES, 2 * half))


def product(place, factor, near, far):
    n = 2 * len(near) * near[0].shape[1]
    return pl.pallas_call(
        functools.partial(product_kernel, len(near)),
        out_shape=jax.ShapeDtypeStruct((n // 2 + SUBLANES, n), F32),
        in_specs=[SMEM] + [VMEM] * (1 + len(near) + len(far)),
        out_specs=VMEM,
        scratch_shapes=[pltpu.VMEM((2 * LANES, 2 * LANES), BF16)],
        compiler_params=SMALL,
        name="product",
    )(place, factor, *near, *far)


def triangle_kernel(scale, gram, out):
    half = gram.shape[1] // 2
    full = opened(gram[:half, :half], gram[:half, half:], gram[half : half + 1, :half])
    upper = joined(eliminated(tiles(full), [[] for _ in range(0, 2 * half, SUBLANES)])[0])
    r, c = triangle_ids(2 * half)
    out[...] = jnp.where(c >= r, upper * scale, 0.0)


def triangle(gram, scale):
    n = gram.shape[1]
    return pl.pallas_call(
        functools.partial(triangle_kernel, scale),
        out_shape=jax.ShapeDtypeStruct((n, n), F32),
        in_specs=[VMEM],
        out_specs=VMEM,
        compiler_params=SMALL,
        name="triangle",
    )(gram)


def local(state_field, start_basis):
    x_cells, y_cells, species, z_cells = state_field.shape
    rank_kept = start_basis.shape[1]
    unfolded = state_field.reshape(x_cells * y_cells * species, z_cells)
    x_parts = lax.axis_size("gx")
    place = lax.axis_index("gx").astype(jnp.int32).reshape(1)
    mine, other, held = local_gram(place, pltpu.with_memory_space_constraint(unfolded, pltpu.HBM))
    mine = summed(mine + partner(other, 1))
    other = partner(mine, 1)
    basis, image, gram = begin(place, mine, other, start_basis.T)
    far = {}
    share = y_cells // x_parts
    for d, skip, count in far_pieces(x_parts, share):
        piece = contract_ahead(place, held, image, x_cells, y_cells, species, share, d, skip, count)
        far[d] = partner(piece, d)
    basis_rows, basis, factor = finish(basis, gram)
    core_tensor, *near = contract(place, held, basis, x_cells, y_cells, species, x_parts)
    near = [partner(piece, d) if d else piece for d, piece in enumerate(near)]
    gram_x = product(place, factor, near, [far[d] for d in sorted(far)])
    gram_x = summed(gram_x + partner(gram_x, 1))
    column_count = y_cells * lax.axis_size("gy") * species * rank_kept
    x_triangle = triangle(gram_x, 1.0 / column_count**0.5)
    return (core_tensor.reshape(x_cells, y_cells, species * rank_kept), basis_rows.T, x_triangle)


def far_pieces(x_parts, share):
    return [(d, 0, share) for d in reversed(range(x_parts // 2, x_parts))]


def solution(mesh):
    return jax.shard_map(
        local,
        mesh=mesh,
        in_specs=(P("gx", "gy", None, None), P()),
        out_specs=(P("gx", "gy", None), P(), P()),
        check_vma=False,
    )
```

```python
import functools

import jax
import jax.numpy as jnp
from jax import lax
from jax.experimental import pallas as pl
from jax.experimental.pallas import tpu as pltpu
from jax.sharding import PartitionSpec as P


ITERS = 3
F32, BF16 = jnp.float32, jnp.bfloat16
LANES, SUBLANES = 128, 8

precise = lax.Precision.HIGHEST
ROWS_BY_ROWS = (((1,), (1,)), ((), ()))
COLUMNS_BY_COLUMNS = (((0,), (0,)), ((), ()))
VMEM = pl.BlockSpec(memory_space=pltpu.VMEM)
SMEM = pl.BlockSpec(memory_space=pltpu.SMEM)
HBM = pl.BlockSpec(memory_space=pltpu.HBM)
SMALL = pltpu.CompilerParams(vmem_limit_bytes=32 << 20)


def bits(size):
    return [1 << b for b in range(size.bit_length() - 1)]


def partner(value, x_mask, y_mask=0):
    x_size, y_size = lax.axis_size("gx"), lax.axis_size("gy")
    pairs = [
        (x * y_size + y, (x ^ x_mask) * y_size + (y ^ y_mask)) for x in range(x_size) for y in range(y_size)
    ]
    return lax.ppermute(value, ("gx", "gy"), pairs)


def summed(value):
    masks = [(bit, 0) for bit in bits(lax.axis_size("gx"))[1:]] + [(0, bit) for bit in bits(lax.axis_size("gy"))]
    while masks:
        first, masks = masks[0], masks[1:]
        near = value + partner(value, *first)
        if masks:
            second, masks = masks[0], masks[1:]
            both = (first[0] ^ second[0], first[1] ^ second[1])
            near = near + (partner(value, *second) + partner(value, *both))
        value = near
    return value


def in_two(value):
    high = value.astype(BF16)
    return high, (value - high.astype(F32)).astype(BF16)


def tiles(value):
    rows, columns = value.shape
    return [
        [value[r : r + SUBLANES, c : min(c + LANES, columns)] for c in range(0, columns, LANES)]
        for r in range(0, rows, SUBLANES)
    ]


def joined(groups):
    return jnp.concatenate([jnp.concatenate(group, axis=1) for group in groups], axis=0)


def eliminated(gram, extra):
    gram = [list(group) for group in gram]
    extra = [list(group) for group in extra]
    row_id = lax.broadcasted_iota(jnp.int32, (SUBLANES, LANES), 0)

    def row(tile, r):
        return jnp.broadcast_to(tile[r : r + 1, :], tile.shape)

    def column(tile, c):
        return jnp.broadcast_to(tile[:, c : c + 1], (SUBLANES, LANES))

    def spread(tile, r):
        return jnp.take_along_axis(tile, jnp.full(tile.shape, r, jnp.int32), axis=0)

    def less(tile, factor, other):
        return tile - factor[:, : tile.shape[1]] * other

    for g in range(len(gram)):
        at, first = divmod(g * SUBLANES, LANES)
        both = [gram[h] + extra[h] for h in range(len(gram))]
        rows = [[row(t, q) for t in both[g]] for q in range(SUBLANES)]
        pivots = [column(gram[g][at], first + b) for b in range(SUBLANES)]
        block = [[spread(pivots[b], a) if b >= a else None for b in range(SUBLANES)] for a in range(SUBLANES)]
        below = range(g + 1, len(gram))
        columns = {h: [column(gram[h][at], first + q) for q in range(SUBLANES)] for h in below}
        scales, inverses = [], []
        for q in range(SUBLANES):
            scales.append(lax.rsqrt(block[q][q]))
            inverses.append(scales[q] * scales[q])
            for b in range(q + 1, SUBLANES):
                factor = block[q][b] * inverses[q]
                for c in range(b, SUBLANES):
                    block[b][c] = block[b][c] - factor * block[q][c]
                rows[b] = [less(t, factor, r) for t, r in zip(rows[b], rows[q])]
                for h in below:
                    columns[h][b] = columns[h][b] - factor * columns[h][q]
        for h in below:
            for q in range(SUBLANES):
                factor = columns[h][q] * inverses[q]
                both[h] = [less(t, factor, r) for t, r in zip(both[h], rows[q])]
        for q in range(SUBLANES):
            both[g] = [
                jnp.where((row_id == q)[:, : t.shape[1]], r * scales[q][:, : t.shape[1]], t)
                for t, r in zip(both[g], rows[q])
            ]
        for h in range(g, len(gram)):
            gram[h], extra[h] = both[h][: len(gram[h])], both[h][len(gram[h]) :]
    return gram, extra


def orth_pass(rows, *more):
    inner_gram = lax.dot_general(rows, rows, ROWS_BY_ROWS, precision=precise, preferred_element_type=F32)
    widths = [v.shape[1] for v in (rows, *more)]
    extra = [sum(parts, []) for parts in zip(*(tiles(v) for v in (rows, *more)))]
    groups = eliminated(tiles(inner_gram), extra)[1]
    out, at = [], 0
    for width in widths:
        count = -(-width // LANES)
        out.append(joined([group[at : at + count] for group in groups]))
        at += count
    return out


def triangle_ids(n):
    return lax.broadcasted_iota(jnp.int32, (n, n), 0), lax.broadcasted_iota(jnp.int32, (n, n), 1)


def folded(full):
    half = full.shape[0] // 2
    r, c = triangle_ids(half)
    corner = full[half:, half:]
    diagonal = jnp.sum(jnp.where(r == c, corner, 0.0), axis=0, keepdims=True)
    return jnp.where(r > c, corner, full[:half, :half]), full[:half, half:], diagonal


def opened(fold, upper, diagonal):
    half = fold.shape[0]
    r, c = triangle_ids(half)
    turned = fold.T
    first = jnp.where(c >= r, fold, turned)
    second = jnp.where(r > c, fold, jnp.where(r == c, jnp.broadcast_to(diagonal, fold.shape), turned))
    return jnp.concatenate(
        [jnp.concatenate([first, upper], axis=1), jnp.concatenate([upper.T, second], axis=1)], axis=0
    )


def species_weights(rows, repeat):
    high, low = in_two(jnp.concatenate([rows] * repeat, axis=0).T)
    weights = jnp.concatenate([high, low], axis=1)
    return jnp.concatenate([weights, weights], axis=0)


def times(value, weights):
    out = jnp.dot(jnp.concatenate(in_two(value), axis=1), weights, preferred_element_type=F32)
    half = out.shape[1] // 2
    return out[:, :half] + out[:, half:]


def gathered(value, rank):
    pack = LANES // rank
    row = lax.broadcasted_iota(jnp.int32, (1, SUBLANES, LANES), 1)
    lane = lax.broadcasted_iota(jnp.int32, (1, SUBLANES, LANES), 2)
    out = value.reshape(value.shape[0] // SUBLANES, SUBLANES, LANES)
    out = jnp.where(row % pack == lane // rank, out, 0.0)
    for bit in bits(pack):
        out = out + pltpu.roll(out, bit, 1)
    return out.reshape(value.shape)


def packed(narrow, first, count, stride, rank):
    return narrow[pl.ds(first + LANES // rank - 1, count, stride=stride), :]


def gram_kernel(cuts, place, field, mine, other, held, arrived):
    copies = [
        pltpu.make_async_copy(field.at[a:b], held.at[a:b], arrived.at[i])
        for i, (a, b) in enumerate(zip(cuts[:-1], cuts[1:]))
    ]
    for copy in copies:
        copy.start()
    total = 0.0
    for copy, a, b in zip(copies, cuts[:-1], cuts[1:]):
        copy.wait()
        high, low = in_two(held[a:b])
        total = total + lax.dot_general(
            high, jnp.concatenate([high, low], axis=1), COLUMNS_BY_COLUMNS, preferred_element_type=F32
        )
    square, cross = jnp.split(total, 2, axis=1)
    fold, upper, diagonal = folded(square + (cross + cross.T))
    half = fold.shape[0]
    edge = SUBLANES
    even = place[0] & 1 == 0

    def put(first, second):
        first[:half] = fold
        first[half:] = upper[:edge]
        second[: half - edge] = upper[edge:]
        second[half - edge :] = jnp.broadcast_to(diagonal, (2 * edge, half))

    @pl.when(even)
    def _():
        put(mine, other)

    @pl.when(jnp.logical_not(even))
    def _():
        put(other, mine)


def local_gram(place, unfolded):
    rows, z = unfolded.shape
    cuts = [0, rows // 8, 3 * rows // 8, 11 * rows // 16, rows]
    out = jax.ShapeDtypeStruct((z // 2 + SUBLANES, z // 2), F32)
    return pl.pallas_call(
        functools.partial(gram_kernel, cuts),
        out_shape=[out, out, jax.ShapeDtypeStruct((rows, z), F32)],
        in_specs=[SMEM, HBM],
        out_specs=[VMEM] * 3,
        scratch_shapes=[pltpu.SemaphoreType.DMA((len(cuts) - 1,))],
        compiler_params=pltpu.CompilerParams(vmem_limit_bytes=32 << 20),
        name="gram",
    )(place, unfolded)


def begin_kernel(place, mine, other, start, basis, image, gram):
    half = mine.shape[1]
    edge = SUBLANES
    even = place[0] & 1 == 0
    first = jnp.where(even, mine[...], other[...])
    second = jnp.where(even, other[...], mine[...])
    gram[...] = opened(
        first[:half],
        jnp.concatenate([first[half:], second[: half - edge]], axis=0),
        second[half - edge : half - edge + 1],
    )
    basis[...] = start[...]

    def multiplied():
        return jnp.dot(basis[...], gram[...], precision=precise, preferred_element_type=F32)

    @pl.loop(0, ITERS - 2)
    def _(iteration):
        basis[...] = orth_pass(*orth_pass(multiplied()))[0]

    basis[...] = orth_pass(multiplied())[0]
    image[...] = multiplied()


def begin(place, mine, other, start_rows):
    z = start_rows.shape[1]
    rows = jax.ShapeDtypeStruct(start_rows.shape, F32)
    return pl.pallas_call(
        begin_kernel,
        out_shape=[rows, rows, jax.ShapeDtypeStruct((z, z), F32)],
        in_specs=[SMEM] + [VMEM] * 3,
        out_specs=[VMEM] * 3,
        compiler_params=SMALL,
        name="begin",
    )(place, mine, other, start_rows)


def finish_kernel(basis, gram, out, again, factor):
    rank = basis.shape[0]
    r, c = triangle_ids(rank)
    rows, turn = orth_pass(basis[...], jnp.where(r == c, 1.0, 0.0))
    rows = jnp.dot(rows, gram[...], precision=precise, preferred_element_type=F32)
    for _ in range(2):
        rows, turn = orth_pass(rows, turn)
    out[...] = rows
    again[...] = rows
    factor[...] = turn


def finish(basis, gram):
    rank, z = basis.shape
    return pl.pallas_call(
        finish_kernel,
        out_shape=[jax.ShapeDtypeStruct((rank, z), F32)] * 2 + [jax.ShapeDtypeStruct((rank, rank), F32)],
        in_specs=[VMEM] * 2,
        out_specs=[VMEM] * 3,
        compiler_params=SMALL,
        cost_estimate=pl.CostEstimate(flops=1 << 30, bytes_accessed=1 << 24, transcendentals=0),
        name="finish",
    )(basis, gram)


def ahead_kernel(d, share, skip, species, place, field, image, out, narrow):
    count, x_cells, width = out.shape
    rank = image.shape[0]
    across = count * species
    start = pl.multiple_of(((place[0] ^ d) * share + skip) * species, species)
    cells = field[:, pl.ds(start, across), :]
    narrow[...] = gathered(
        times(cells.reshape(x_cells * across, cells.shape[2]), species_weights(image[...], LANES // rank)), rank
    )
    for y in range(count):
        for t in range(width // LANES):
            out[y, :, t * LANES : (t + 1) * LANES] = packed(
                narrow, y * species + t * (LANES // rank), x_cells, across, rank
            )


def contract_ahead(place, field, image, x_cells, y_cells, species, share, d, skip, count):
    z = field.shape[1]
    rank = image.shape[0]
    return pl.pallas_call(
        functools.partial(ahead_kernel, d, share, skip, species),
        out_shape=jax.ShapeDtypeStruct((count, x_cells, species * rank), F32),
        in_specs=[SMEM, VMEM, VMEM],
        out_specs=VMEM,
        scratch_shapes=[pltpu.VMEM((x_cells * count * species, LANES), F32)],
        compiler_params=SMALL,
        cost_estimate=pl.CostEstimate(flops=1 << 30, bytes_accessed=1 << 22, transcendentals=0),
    )(place, field.reshape(x_cells, y_cells * species, z), image)


def core_kernel(species, y_cells, place, field, basis, core, *refs):
    outs, (weights, narrow, strip) = refs[:-3], refs[-3:]
    share, step, width = outs[0].shape
    rank = basis.shape[0]
    cells = core.shape[0]
    half = len(outs)
    near = place[0] // half * half

    @pl.when(pl.program_id(0) == 0)
    def _():
        weights[...] = species_weights(basis[...], LANES // rank)

    block = narrow.shape[0]
    cells_of_step = field[pl.ds(pl.multiple_of(pl.program_id(0) * block, block), block), :]
    narrow[...] = gathered(times(cells_of_step, weights[...]), rank)
    for t in range(width // LANES):
        lanes = slice(t * LANES, (t + 1) * LANES)
        strip[...] = packed(narrow, t * (LANES // rank), cells, species, rank)
        core[:, lanes] = strip[...]
        for d, out in enumerate(outs):
            part = near + ((place[0] ^ d) & (half - 1))
            for y in range(share):
                out[y, :, lanes] = strip[pl.ds(part * share + y, step, stride=y_cells), :]


def contract(place, unfolded, basis, x_cells, y_cells, species, x_parts):
    rows, z = unfolded.shape
    rank = basis.shape[0]
    steps = 4
    block, cells = rows // steps, rows // species // steps
    width = species * rank
    share = y_cells // x_parts
    pieces = x_parts // 2
    return pl.pallas_call(
        functools.partial(core_kernel, species, y_cells),
        grid=(steps,),
        out_shape=[jax.ShapeDtypeStruct((rows // species, width), F32)]
        + [jax.ShapeDtypeStruct((share, x_cells, width), F32)] * pieces,
        in_specs=[
            SMEM,
            VMEM,
            pl.BlockSpec((rank, z), lambda i: (0, 0)),
        ],
        out_specs=[pl.BlockSpec((cells, width), lambda i: (i, 0))]
        + [pl.BlockSpec((share, x_cells // steps, width), lambda i: (0, i, 0))] * pieces,
        scratch_shapes=[
            pltpu.VMEM((2 * z, 2 * LANES), BF16),
            pltpu.VMEM((block, LANES), F32),
            pltpu.VMEM((cells, LANES), F32),
        ],
        compiler_params=SMALL,
        cost_estimate=pl.CostEstimate(flops=1 << 31, bytes_accessed=1 << 24, transcendentals=0),
        name="core",
    )(place, unfolded, basis)


def product_kernel(near_count, place, factor, *refs):
    near, far, (out, turn) = refs[:near_count], refs[near_count:-2], refs[-2:]
    share, size, width = near[0].shape
    rank = factor.shape[0]
    turn[...] = jnp.zeros_like(turn)
    for part, value in enumerate(in_two(factor[...])):
        for side in range(2):
            for q in range(LANES // rank):
                turn[
                    part * LANES + q * rank : part * LANES + (q + 1) * rank,
                    side * LANES + q * rank : side * LANES + (q + 1) * rank,
                ] = value
    strips = [
        piece[y, :, t : t + LANES]
        for piece in far
        for y in range(piece.shape[0])
        for t in range(0, width, LANES)
    ]
    both = jnp.concatenate(in_two(jnp.concatenate(strips, axis=0)), axis=1)
    turned = lax.dot_general(both, turn[...], ROWS_BY_ROWS, preferred_element_type=F32)
    turned = turned[:, :LANES] + turned[:, LANES:]
    count = width // LANES
    columns = []
    for y in range(share):
        rows = [piece[y] for piece in near]
        for d in range(near_count):
            at = (d * share + y) * count
            rows.append(
                jnp.concatenate([turned[(at + t) * size : (at + t + 1) * size] for t in range(count)], axis=1)
            )
        columns.append(jnp.concatenate(rows, axis=0))
    high, low = in_two(jnp.concatenate(columns, axis=1))
    total = lax.dot_general(
        high, jnp.concatenate([high, low], axis=0), ROWS_BY_ROWS, preferred_element_type=F32
    )
    square, cross = jnp.split(total, 2, axis=1)
    total = square + (cross + cross.T)
    for bit in bits(2 * near_count):
        step = size * bit
        swap = place[0] & bit != 0
        for axis in (0, 1):
            parts = [lax.slice_in_dim(total, c, c + step, axis=axis) for c in range(0, total.shape[axis], step)]
            swapped = jnp.concatenate([parts[c ^ 1] for c in range(len(parts))], axis=axis)
            total = jnp.where(swap, swapped, total)
    fold, upper, diagonal = folded(total)
    half = fold.shape[0]
    out[:half] = jnp.concatenate([fold, upper], axis=1)
    out[half:] = jnp.broadcast_to(jnp.concatenate([diagonal, diagonal], axis=1), (SUBLANES, 2 * half))


def product(place, factor, near, far):
    n = 2 * len(near) * near[0].shape[1]
    return pl.pallas_call(
        functools.partial(product_kernel, len(near)),
        out_shape=jax.ShapeDtypeStruct((n // 2 + SUBLANES, n), F32),
        in_specs=[SMEM] + [VMEM] * (1 + len(near) + len(far)),
        out_specs=VMEM,
        scratch_shapes=[pltpu.VMEM((2 * LANES, 2 * LANES), BF16)],
        compiler_params=SMALL,
        name="product",
    )(place, factor, *near, *far)


def triangle_kernel(scale, gram, out):
    half = gram.shape[1] // 2
    full = opened(gram[:half, :half], gram[:half, half:], gram[half : half + 1, :half])
    upper = joined(eliminated(tiles(full), [[] for _ in range(0, 2 * half, SUBLANES)])[0])
    r, c = triangle_ids(2 * half)
    out[...] = jnp.where(c >= r, upper * scale, 0.0)


def triangle(gram, scale):
    n = gram.shape[1]
    return pl.pallas_call(
        functools.partial(triangle_kernel, scale),
        out_shape=jax.ShapeDtypeStruct((n, n), F32),
        in_specs=[VMEM],
        out_specs=VMEM,
        compiler_params=SMALL,
        name="triangle",
    )(gram)


def local(state_field, start_basis):
    x_cells, y_cells, species, z_cells = state_field.shape
    rank_kept = start_basis.shape[1]
    unfolded = state_field.reshape(x_cells * y_cells * species, z_cells)
    x_parts = lax.axis_size("gx")
    place = lax.axis_index("gx").astype(jnp.int32).reshape(1)
    mine, other, held = local_gram(place, pltpu.with_memory_space_constraint(unfolded, pltpu.HBM))
    mine = summed(mine + partner(other, 1))
    other = partner(mine, 1)
    basis, image, gram = begin(place, mine, other, start_basis.T)
    far = []
    share = y_cells // x_parts
    for d, skip, count in far_pieces(x_parts, share):
        piece = contract_ahead(place, held, image, x_cells, y_cells, species, share, d, skip, count)
        far.append(partner(piece, d))
    basis_rows, basis, factor = finish(basis, gram)
    core_tensor, *near = contract(place, held, basis, x_cells, y_cells, species, x_parts)
    near = [partner(piece, d) if d else piece for d, piece in enumerate(near)]
    gram_x = product(place, factor, near, far)
    gram_x = summed(gram_x + partner(gram_x, 1))
    column_count = y_cells * lax.axis_size("gy") * species * rank_kept
    x_triangle = triangle(gram_x, 1.0 / column_count**0.5)
    return (core_tensor.reshape(x_cells, y_cells, species * rank_kept), basis_rows.T, x_triangle)


def far_pieces(x_parts, share):
    return [(d, 0, share) for d in range(x_parts // 2, x_parts)]


def solution(mesh):
    return jax.shard_map(
        local,
        mesh=mesh,
        in_specs=(P("gx", "gy", None, None), P()),
        out_specs=(P("gx", "gy", None), P(), P()),
        check_vma=False,
    )
```
